1024 devices in a mesh: replica: 64 (over y_hi, z, core), shard: 16 (over x, y_lo).
Axes of the slice: x: 4, y: 8 (y_hi: 2, y_lo: 4; y = y_hi * 4 + y_lo), z: 16, core: 2. Of those that a mesh axis runs over, the one named last changes fastest.
Arguments:
- dec_grad: bfloat16 [1024, 16, 8192], P(('replica', 'shard')), may hold values from -0.25 to 0.25
- dec_master: float32 [16, 8192], P('shard'), may hold values from -6 to 6
- dec_moment: float32 [16, 8192], P('shard'), may hold values from -2 to 2
- dec_second: float32 [16, 8192], P('shard'), may hold values from 0.01 to 1
- vis_grad: bfloat16 [1024, 1280, 128], P(('replica', 'shard')), may hold values from -0.75 to 0.75
- vis_owner: int32 [1280], replicated, may hold values from 0 to 15, as said below
- vis_master: float32 [2560, 128], P('shard'), may hold values from -6 to 6
- vis_moment: float32 [2560, 128], P('shard'), may hold values from -2 to 2
- vis_second: float32 [2560, 128], P('shard'), may hold values from 0.01 to 1
- step_count: int32 [1], replicated, may hold values from 1 to 4096
Outputs:
- dec_master_new: float32 [16, 8192], P('shard')
- dec_moment_new: float32 [16, 8192], P('shard')
- dec_second_new: float32 [16, 8192], P('shard')
- dec_weight: bfloat16 [16, 8192], replicated
- vis_master_new: float32 [2560, 128], P('shard')
- vis_moment_new: float32 [2560, 128], P('shard')
- vis_second_new: float32 [2560, 128], P('shard')
- vis_weight: bfloat16 [1280, 128], replicated
The draws below stay inside these ranges and needn't reach their ends.
Inputs may be any that keep to these rules, and one draw needn't show every extreme that they name: `vis_owner`: within each aligned range of 80 blocks, no owner receives more than 10 blocks; one owner, drawn afresh, receives exactly 10 blocks from every range and so 160 blocks in all.
All inputs are finite; a program needn't handle non-finite values.
Results may differ from the reference program's by a relative error of at most 0.001.
Values may be sent and summed in bfloat16 or wider, within the bound.
A program may use at most 32 MiB of HBM per device.

```python
import math
import jax
import jax.numpy as jnp
from jax import lax

D = 8192
VW = 128
VB_DEV = 80
DEC_ROWS = 16
VIS_BLOCKS = 1280
SRC_CAP = 10
CAP = 160
N_REPLICA = 64
N_SHARD = 16


def draw_vis_owner(key, part):
    hot_key, rest_key = jax.random.split(jax.random.fold_in(key, 7))
    hottest = jax.random.randint(hot_key, (), 0, N_SHARD).astype(jnp.int32)

    def one_range(range_key):
        first_key, second_key = jax.random.split(range_key)
        order = jax.random.permutation(first_key, VB_DEV)
        others = jnp.arange((N_SHARD - 1) * SRC_CAP, dtype=jnp.int32) // SRC_CAP
        others = jax.random.permutation(second_key, others)
        others = jnp.where(others >= hottest, others + 1, others).astype(jnp.int32)
        labels = jnp.concatenate([jnp.full((SRC_CAP,), hottest, jnp.int32), others[:VB_DEV - SRC_CAP]])
        return jnp.zeros((VB_DEV,), jnp.int32).at[order].set(labels)
    range_keys = jax.random.split(rest_key, N_SHARD)
    return jax.vmap(one_range)(range_keys).reshape(-1)


def raised(entries, own_key, source, target, blocks, factor):
    owner, partner = [(jnp.arange(entries.shape[dim]) // (entries.shape[dim] // blocks)).reshape([-1 if axis == dim else 1 for axis in range(entries.ndim)]) for dim in (source, target)]
    chosen = jax.random.permutation(own_key, blocks)[partner]
    strong = (owner == chosen) | (owner == (partner + blocks // 2) % blocks)
    return jnp.where(strong, factor * entries, entries)


def steps_of(own_key, extent, pieces, smallest, largest):
    def one(dim, parts):
        steps = jax.random.uniform(jax.random.fold_in(jax.random.fold_in(own_key, 6), dim), (parts,), jnp.float32, smallest / len(pieces), largest / len(pieces))
        return jnp.repeat(jnp.exp(steps), extent[dim] // parts).reshape((-1,) + (1,) * (len(extent) - dim - 1))

    gain = one(*pieces[0])
    for cut in pieces[1:]:
        gain = gain * one(*cut)
    return gain


def noise(key, dims, deviation, bound, cuts=(), kind=jnp.bfloat16):
    array = deviation * jax.random.normal(key, dims, jnp.float32)
    if cuts:
        array = array * steps_of(key, dims, cuts, -0.22, 0.18)
    return jnp.clip(array, -bound, bound).astype(kind)


def bell_draw_with(own_key, dims, deviation, most, pieces, heavy, kind=jnp.bfloat16):
    result = deviation * jax.random.normal(own_key, dims, jnp.float32)
    if pieces:
        result = result * steps_of(own_key, dims, pieces, -0.22, 0.18)
    return jnp.clip(raised(result, jax.random.fold_in(own_key, 3), *heavy), -most, most).astype(kind)


def setup_inputs(seed: int = 0) -> dict:
    keys = jax.random.split(jax.random.key(seed), 11)
    return {
        "dec_grad": bell_draw_with(keys[0], (N_REPLICA * N_SHARD, DEC_ROWS, D), 0.03125, 0.25, ((0, 1024),), (0, 1, 16, 2.0)),
        "dec_master": noise(keys[1], (DEC_ROWS, D), 1.0, 6.0, ((0, 16),), jnp.float32),
        "dec_moment": noise(keys[2], (DEC_ROWS, D), 0.3, 2.0, ((0, 16),), jnp.float32),
        "dec_second": jnp.clip(jnp.exp(math.log(1.0) - 4.6051702 * jax.random.uniform(keys[3], (DEC_ROWS, D), jnp.float32) ** steps_of(keys[3], (DEC_ROWS, D), ((0, 16),), -0.2, 0.2)), 0.01, 1.0),
        "vis_grad": bell_draw_with(keys[4], (N_REPLICA * N_SHARD, VIS_BLOCKS, VW), 0.03125, 0.75, ((0, 1024),), (0, 1, 256, 6.0)),
        "vis_owner": draw_vis_owner(jax.random.fold_in(keys[10], 71), 0),
        "vis_master": noise(keys[6], (N_SHARD * CAP, VW), 1.0, 6.0, ((0, 16),), jnp.float32),
        "vis_moment": noise(keys[7], (N_SHARD * CAP, VW), 0.3, 2.0, ((0, 16),), jnp.float32),
        "vis_second": jnp.clip(jnp.exp(math.log(1.0) - 4.6051702 * jax.random.uniform(keys[8], (N_SHARD * CAP, VW), jnp.float32) ** steps_of(keys[8], (N_SHARD * CAP, VW), ((0, 16),), -0.2, 0.2)), 0.01, 1.0),
        "step_count": jax.random.randint(keys[9], (1,), 1, 4097).astype(jnp.int32),
    }


beta_one = 0.9
beta_two = 0.999
learn_rate = 0.02
weight_decay = 0.1
epsilon = 1e-08

def summed(gradient):
    term_count = gradient.shape[0]
    group_size = 32 if term_count % 32 == 0 else 1
    grouped_terms = gradient.reshape((term_count // group_size, group_size) + gradient.shape[1:])

    def add_terms(running, term_block):
        return (running + lax.optimization_barrier(jnp.sum(term_block.astype(jnp.float32), axis=0)), None)
    running, unused = lax.scan(add_terms, jnp.zeros(gradient.shape[1:], jnp.float32), grouped_terms)
    return running

def place_blocks(owner_map, range_size, per_source, owners):
    grouped = owner_map.reshape(-1, range_size)
    onehot = (grouped[:, :, None] == jnp.arange(owners, dtype=jnp.int32)[None, None, :]).astype(jnp.int32)
    position = lax.optimization_barrier(jnp.sum((jnp.cumsum(onehot, axis=1) - onehot) * onehot, axis=2))
    source = jnp.arange(grouped.shape[0], dtype=jnp.int32)[:, None]
    return (grouped * (owners * per_source) + source * per_source + position).reshape(-1).astype(jnp.int32)

def adamw(gradient, moment, second, master, step_count):
    step_float = step_count[0].astype(jnp.float32)
    fix_one = 1.0 - jnp.power(beta_one, step_float)
    fix_two = 1.0 - jnp.power(beta_two, step_float)
    moment = beta_one * moment + (1.0 - beta_one) * gradient
    second = beta_two * second + (1.0 - beta_two) * gradient * gradient
    master = master - learn_rate * (moment / fix_one / (jnp.sqrt(second / fix_two) + epsilon) + weight_decay * master)
    return (moment, second, master)

def reference(dec_grad, dec_master, dec_moment, dec_second, vis_grad, vis_owner, vis_master, vis_moment, vis_second, step_count):
    dec_sum = summed(dec_grad)
    vis_sum = summed(vis_grad)
    row_of = place_blocks(vis_owner, VB_DEV, SRC_CAP, N_SHARD)
    vis_rows = jnp.zeros(vis_master.shape, jnp.float32).at[row_of].set(vis_sum)
    dec_moment_new, dec_second_new, dec_master_new = adamw(dec_sum, dec_moment, dec_second, dec_master, step_count)
    vis_moment_new, vis_second_new, vis_master_new = adamw(vis_rows, vis_moment, vis_second, vis_master, step_count)
    dec_weight = dec_master_new.astype(jnp.bfloat16)
    vis_weight = vis_master_new[row_of].astype(jnp.bfloat16)
    return (dec_master_new, dec_moment_new, dec_second_new, dec_weight, vis_master_new, vis_moment_new, vis_second_new, vis_weight)
```

```python
import math

import jax
import jax.numpy as jnp
from jax import lax
from jax.experimental import pallas as pl
from jax.experimental.pallas import tpu as pltpu
from jax.sharding import PartitionSpec as P

beta_one = 0.9
beta_two = 0.999
learn_rate = 0.02
weight_decay = 0.1
epsilon = 1e-08

MESH = pl.DeviceIdType.MESH
F32 = jnp.float32
BF16 = jnp.bfloat16
HIGH = lax.Precision.HIGHEST

NX, NY, NZ = 4, 8, 16
Q = 4
ROWS = 80
DEC = 64
PAD = 96
PART = PAD // 4
SLOT = 16
USED = 10
CAP = 160


def adamw(g, m, v, p, inv_one, inv_two):
    m = beta_one * m + (1.0 - beta_one) * g
    v = beta_two * v + (1.0 - beta_two) * g * g
    p = p - learn_rate * (m * inv_one / (jnp.sqrt(v * inv_two) + epsilon) + weight_decay * p)
    return m, v, p


def kernel(
    step_ref,
    own_ref,
    dec_grad,
    vis_grad,
    dec_p,
    dec_m,
    dec_v,
    vis_p,
    vis_m,
    vis_v,
    o_dp,
    o_dm,
    o_dv,
    o_dw,
    o_vp,
    o_vm,
    o_vv,
    o_vw,
    a_dec,
    b_dec,
    a_vis,
    b_vis,
    s_dec,
    s_vis,
    acc,
    ry,
    ay,
    rx,
    ax,
    rz,
    az,
    ryh,
    ah,
    rzh,
    tz,
    g4,
    gdec,
    wall,
    st,
    stm,
    stx,
    gx,
    gm,
    gr,
    n_dec,
    n_vis,
    wide,
    dw,
    lsem,
    ssem,
    rsem,
):
    rep, sh = lax.axis_index("replica"), lax.axis_index("shard")
    core = lax.rem(rep, 2)
    z = lax.rem(rep // 2, NZ)
    yl = lax.rem(sh, Q)
    y = (rep // (2 * NZ)) * Q + yl
    x = sh // Q
    zq = lax.rem(z, 4)

    def dev(dx=0, dy=0, dz=0, dc=0):
        xx = lax.rem(x + dx + NX, NX)
        yy = lax.rem(y + dy + NY, NY)
        zz = lax.rem(z + dz + NZ, NZ)
        cc = lax.rem(core + dc, 2)
        return ((yy // Q) * NZ + zz) * 2 + cc, xx * Q + lax.rem(yy, Q)

    def at4(i, d):
        return lax.rem(i + d + 4, 4)

    used = [0]

    def remote(src, dst, target):
        k = used[0]
        used[0] += 1
        return pltpu.make_async_remote_copy(
            src_ref=src,
            dst_ref=dst,
            send_sem=ssem.at[k],
            recv_sem=rsem.at[k],
            device_id=target,
            device_id_type=MESH,
        )

    locals_used = [0]

    def local(src, dst):
        k = locals_used[0]
        locals_used[0] += 1
        return pltpu.make_async_copy(src, dst, lsem.at[k])

    def go(copies):
        for c in copies:
            c.start()

    def done(copies):
        for c in copies:
            c.wait()

    is_dec, is_vis = core == 0, core == 1

    load_dec = local(dec_grad.at[0], a_dec)
    load_vis = local(vis_grad.at[0], a_vis)
    load_state = [
        local(src, dst)
        for src, dst in (
            (dec_p, s_dec.at[0]),
            (dec_m, s_dec.at[1]),
            (dec_v, s_dec.at[2]),
            (vis_p, s_vis.at[0]),
            (vis_m, s_vis.at[1]),
            (vis_v, s_vis.at[2]),
        )
    ]

    @pl.when(is_dec)
    def _():
        load_dec.start()

    @pl.when(is_vis)
    def _():
        load_vis.start()

    go(load_state)

    friends = [dev(dc=1)]
    friends += [dev(dx=d) for d in (1, -1, 2)]
    friends += [dev(dy=d) for d in (1, -1, 2, -2, 4)]
    friends += [dev(dz=d) for d in (1, -1, 2, -2, 4, -4, 8)]
    barrier = pltpu.get_barrier_semaphore()
    for friend in friends:
        pl.semaphore_signal(barrier, inc=1, device_id=friend, device_id_type=MESH)
    pl.semaphore_wait(barrier, len(friends))

    send_vis = remote(vis_grad.at[0], b_vis, dev(dc=1))
    send_dec = remote(dec_grad.at[0], b_dec, dev(dc=1))

    @pl.when(is_dec)
    def _():
        send_vis.start()
        load_dec.wait()
        send_dec.wait_recv()

        @pl.loop(0, DEC)
        def _(j):
            at = pl.multiple_of(j * 128, 128)
            block = a_dec[:, pl.ds(at, 128)].astype(F32) + b_dec[:, pl.ds(at, 128)].astype(F32)
            acc.reshape(16 * ROWS, 128)[pl.ds(j, 16, stride=ROWS), :] = block

        for i in range(16):
            acc[i // 4, i % 4, DEC:ROWS, :] = jnp.zeros((ROWS - DEC, 128), F32)
        send_vis.wait_send()

    @pl.when(is_vis)
    def _():
        send_dec.start()
        load_vis.wait()
        send_vis.wait_recv()

        for i in range(16):
            part = pl.ds(i * ROWS, ROWS)
            acc[i // 4, i % 4] = a_vis[part, :].astype(F32) + b_vis[part, :].astype(F32)
        send_dec.wait_send()

    q1, q2, q3 = at4(yl, 1), at4(yl, 2), at4(yl, 3)
    lo, hi = pl.ds(0, 2), pl.ds(2, 2)
    copies = [
        remote(acc.at[lo, q2], ry.at[2, lo], dev(dy=2)),
        remote(acc.at[hi, q2], ry.at[2, hi], dev(dy=-2)),
        remote(acc.at[:, q1], ry.at[0], dev(dy=1)),
        remote(acc.at[:, q3], ry.at[1], dev(dy=-1)),
    ]
    go(copies)
    done(copies)
    for i in range(NX):
        ay[i] = (acc[i, yl] + ry[0, i]) + (ry[1, i] + ry[2, i])

    copies = [
        remote(ay.at[at4(x, 2)], rx.at[2], dev(dx=2)),
        remote(ay.at[at4(x, 1)], rx.at[0], dev(dx=1)),
        remote(ay.at[at4(x, 3)], rx.at[1], dev(dx=-1)),
    ]
    go(copies)
    done(copies)
    ax[0:ROWS, :] = (ay[x] + rx[0]) + (rx[1] + rx[2])
    ax[ROWS:PAD, :] = jnp.zeros((PAD - ROWS, 128), F32)

    def part_of(i):
        return pl.ds(pl.multiple_of(i * PART, 8), PART)

    copies = [
        remote(ax.at[part_of(at4(zq, 2))], rz.at[2], dev(dz=2)),
        remote(ax.at[part_of(at4(zq, 1))], rz.at[0], dev(dz=1)),
        remote(ax.at[part_of(at4(zq, 3))], rz.at[1], dev(dz=-1)),
    ]
    go(copies)

    done(load_state)
    for i in range(16):
        for k in range(3):
            st[i, k * SLOT : k * SLOT + SLOT, :] = jnp.zeros((SLOT, 128), F32)
            st[i, k * SLOT : k * SLOT + USED, :] = s_vis[k, i * USED : i * USED + USED, :]

    def along_x(src, dst):
        return [
            remote(src.at[pl.ds(at4(x, d) * 4, 4)], dst.at[x], dev(dx=e))
            for d, e in ((2, 2), (1, 1), (3, -1))
        ]

    def along_y(src, dst):
        return [
            remote(src.at[:, at4(yl, d)], dst.at[:, yl], dev(dy=e))
            for d, e in ((2, 2), (1, 1), (3, -1))
        ]

    st_x = along_x(st, stm)
    st_y = along_y(stm, stx)
    back = [at4(x, d) for d in (-2, -1, 1)]

    @pl.when(is_vis)
    def _():
        go(st_x)
        stm[x] = st[pl.ds(x * 4, 4)]

    done(copies)
    az[...] = (ax[part_of(zq), :] + rz[0]) + (rz[1] + rz[2])

    far = remote(az, ryh, dev(dy=4))
    far.start()

    @pl.when(is_vis)
    def _():
        done(st_x)

    far.wait()
    ah[...] = az[...] + ryh[...]
    copies = [
        remote(ah, rzh.at[2], dev(dz=8)),
        remote(ah, rzh.at[0], dev(dz=4)),
        remote(ah, rzh.at[1], dev(dz=-4)),
    ]
    go(copies)

    @pl.when(is_vis)
    def _():
        go(st_y)
        stx[:, yl] = stm[:, yl]

    t = jnp.full((1, 128), step_ref[0].astype(F32), F32)
    inv_one = 1.0 / (1.0 - jnp.exp(t * math.log(beta_one)))
    inv_two = 1.0 / (1.0 - jnp.exp(t * math.log(beta_two)))

    own = own_ref[pl.ds(sh, 1), :]
    one_hot = (lax.broadcasted_iota(jnp.int32, (16, ROWS), 0) == own).astype(F32)
    before = (
        lax.broadcasted_iota(jnp.int32, (ROWS, ROWS), 0)
        < lax.broadcasted_iota(jnp.int32, (ROWS, ROWS), 1)
    ).astype(F32)
    count = jnp.dot(one_hot, before, preferred_element_type=F32)
    position = jnp.sum(one_hot * count, axis=0, keepdims=True)
    key = own * SLOT + position.astype(jnp.int32)
    pick = (lax.broadcasted_iota(jnp.int32, (16 * SLOT, ROWS), 0) == key).astype(F32)

    def blocks_of(k):
        rows = stx[:, :, k * SLOT : k * SLOT + SLOT, :].reshape(16 * SLOT, 128)
        return lax.dot_general(
            pick, rows, (((0,), (0,)), ((), ())), precision=HIGH, preferred_element_type=F32
        )

    @pl.when(is_vis)
    def _():
        done(st_y)
        for k in range(3):
            n_vis[k, 0:ROWS, :] = blocks_of(k)

    done(copies)
    tz[...] = (ah[...] + rzh[2]) + (rzh[0] + rzh[1])

    copies = [
        remote(tz, g4.at[zq], dev(dz=2)),
        remote(tz, g4.at[zq], dev(dz=1)),
        remote(tz, g4.at[zq], dev(dz=-1)),
    ]
    go(copies)
    g4[zq] = tz[...]
    done(copies)

    g_x = along_x(gx, gm)
    g_y = along_y(gm, gr)
    dec_over = remote(gdec, gdec, dev(dc=1))
    vis_over = remote(gr, gr, dev(dc=1))

    @pl.when(is_dec)
    def _():
        g = g4[...].reshape(PAD, 128)[0:DEC]
        gdec[...] = g
        dec_over.start()
        _, _, p = adamw(g, s_dec[1], s_dec[2], s_dec[0], inv_one, inv_two)
        wall[x, yl, 0:DEC, :] = p.astype(BF16)
        wall[x, yl, DEC:ROWS, :] = jnp.zeros((ROWS - DEC, 128), BF16)

    @pl.when(is_vis)
    def _():
        g = g4[...].reshape(PAD, 128)[0:ROWS]
        _, _, p = adamw(
            g, n_vis[1, 0:ROWS, :], n_vis[2, 0:ROWS, :], n_vis[0, 0:ROWS, :], inv_one, inv_two
        )
        wall[x, yl] = p.astype(BF16)

    w_x = [remote(wall.at[x, yl], wall.at[x, yl], dev(dx=d)) for d in (2, 1, -1)]
    go(w_x)

    @pl.when(is_vis)
    def _():
        g = g4[...].reshape(PAD, 128)[0:ROWS]
        rows = jnp.dot(pick, g, precision=HIGH, preferred_element_type=F32)
        gx[...] = rows.reshape(16, SLOT, 128)
        go(g_x)
        gm[x] = gx[pl.ds(x * 4, 4)]

    done(w_x)
    w_y = [
        remote(wall.at[lo, yl], wall.at[lo, yl], dev(dy=2)),
        remote(wall.at[hi, yl], wall.at[hi, yl], dev(dy=-2)),
        remote(wall.at[:, yl], wall.at[:, yl], dev(dy=1)),
        remote(wall.at[:, yl], wall.at[:, yl], dev(dy=-1)),
    ]
    go(w_y)

    outs_dec = [local(n_dec.at[k], o) for k, o in enumerate((o_dp, o_dm, o_dv))]
    outs_vis = [local(n_vis.at[k], o) for k, o in enumerate((o_vp, o_vm, o_vv))]

    @pl.when(is_vis)
    def _():
        done(g_x)
        go(g_y)
        gr[:, yl] = gm[:, yl]
        dec_over.wait_recv()

    m, v, p = adamw(gdec[...], s_dec[1], s_dec[2], s_dec[0], inv_one, inv_two)
    n_dec[0], n_dec[1], n_dec[2] = p, m, v
    go(outs_dec)

    @pl.when(is_vis)
    def _():
        done(g_y)
        vis_over.start()

    @pl.when(is_dec)
    def _():
        vis_over.wait_recv()

    for i in range(16):
        part = pl.ds(i * USED, USED)
        g = gr[i // 4, i % 4, 0:USED, :]
        m, v, p = adamw(
            g, s_vis[1, part, :], s_vis[2, part, :], s_vis[0, part, :], inv_one, inv_two
        )
        n_vis[0, part, :] = p
        n_vis[1, part, :] = m
        n_vis[2, part, :] = v
    go(outs_vis)
    done(w_y)

    out_vw, out_dw = local(wall.reshape(16 * ROWS, 128), o_vw), local(dw, o_dw)
    over_vw = remote(wall.reshape(16 * ROWS, 128), o_vw, dev(dc=1))
    over_dw = remote(dw, o_dw, dev(dc=1))

    @pl.when(is_vis)
    def _():
        over_vw.start()
        out_vw.start()
        over_dw.wait_recv()
        out_vw.wait()
        over_vw.wait_send()
        vis_over.wait_send()

    @pl.when(is_dec)
    def _():
        for i in range(16):
            wide[i * DEC : i * DEC + DEC, :] = wall[i // 4, i % 4, 0:DEC, :].astype(F32)

        @pl.loop(0, DEC)
        def _(j):
            at = pl.multiple_of(j * 128, 128)
            dw[:, pl.ds(at, 128)] = wide[pl.ds(j, 16, stride=DEC), :].astype(BF16)

        over_dw.start()
        out_dw.start()
        over_vw.wait_recv()
        out_dw.wait()
        over_dw.wait_send()
        dec_over.wait_send()

    done(outs_dec)
    done(outs_vis)


def body(
    dec_grad,
    dec_master,
    dec_moment,
    dec_second,
    vis_grad,
    vis_owner,
    vis_master,
    vis_moment,
    vis_second,
    step_count,
):
    anywhere = pl.BlockSpec(memory_space=pl.ANY)
    sds = jax.ShapeDtypeStruct
    vmem = pltpu.VMEM
    out_shape = [
        sds((DEC, 128), F32),
        sds((DEC, 128), F32),
        sds((DEC, 128), F32),
        sds((16, DEC * 128), BF16),
        sds((CAP, 128), F32),
        sds((CAP, 128), F32),
        sds((CAP, 128), F32),
        sds((16 * ROWS, 128), BF16),
    ]
    scratch = [
        vmem((16, DEC * 128), BF16),
        vmem((16, DEC * 128), BF16),
        vmem((16 * ROWS, 128), BF16),
        vmem((16 * ROWS, 128), BF16),
        vmem((3, DEC, 128), F32),
        vmem((3, CAP, 128), F32),
        vmem((4, 4, ROWS, 128), F32),
        vmem((3, 4, ROWS, 128), F32),
        vmem((4, ROWS, 128), F32),
        vmem((3, ROWS, 128), F32),
        vmem((PAD, 128), F32),
        vmem((3, PART, 128), F32),
        vmem((PART, 128), F32),
        vmem((PART, 128), F32),
        vmem((PART, 128), F32),
        vmem((3, PART, 128), F32),
        vmem((PART, 128), F32),
        vmem((4, PART, 128), F32),
        vmem((DEC, 128), F32),
        vmem((4, 4, ROWS, 128), BF16),
        vmem((16, 3 * SLOT, 128), F32),
        vmem((4, 4, 3 * SLOT, 128), F32),
        vmem((4, 4, 3 * SLOT, 128), F32),
        vmem((16, SLOT, 128), F32),
        vmem((4, 4, SLOT, 128), F32),
        vmem((4, 4, SLOT, 128), F32),
        vmem((3, DEC, 128), F32),
        vmem((3, CAP, 128), F32),
        vmem((16 * DEC, 128), F32),
        vmem((16, DEC * 128), BF16),
        pltpu.SemaphoreType.DMA((20,)),
        pltpu.SemaphoreType.DMA((64,)),
        pltpu.SemaphoreType.DMA((64,)),
    ]
    outs = pl.pallas_call(
        kernel,
        out_shape=out_shape,
        in_specs=[pl.BlockSpec(memory_space=pltpu.SMEM), pl.BlockSpec(memory_space=pltpu.VMEM)]
        + [anywhere] * 8,
        out_specs=[anywhere] * 8,
        scratch_shapes=scratch,
        compiler_params=pltpu.CompilerParams(collective_id=0, has_side_effects=True),
    )(
        step_count,
        vis_owner.reshape(16, ROWS),
        dec_grad,
        vis_grad,
        dec_master.reshape(DEC, 128),
        dec_moment.reshape(DEC, 128),
        dec_second.reshape(DEC, 128),
        vis_master,
        vis_moment,
        vis_second,
    )
    outs = list(outs)
    for i in range(3):
        outs[i] = outs[i].reshape(1, DEC * 128)
    return tuple(outs)


def solution(mesh):
    in_specs = (
        P(("replica", "shard"), None, None),
        P("shard", None),
        P("shard", None),
        P("shard", None),
        P(("replica", "shard"), None, None),
        P(),
        P("shard", None),
        P("shard", None),
        P("shard", None),
        P(),
    )
    out_specs = (
        P("shard", None),
        P("shard", None),
        P("shard", None),
        P(),
        P("shard", None),
        P("shard", None),
        P("shard", None),
        P(),
    )
    return jax.shard_map(body, mesh=mesh, in_specs=in_specs, out_specs=out_specs, check_vma=False)
```

```python
import itertools
import math

import jax
import jax.numpy as jnp
from jax import lax
from jax.experimental import pallas as pl
from jax.experimental.pallas import tpu as pltpu
from jax.sharding import PartitionSpec as P

beta_one = 0.9
beta_two = 0.999
learn_rate = 0.02
weight_decay = 0.1
epsilon = 1e-08

MESH = pl.DeviceIdType.MESH
F32 = jnp.float32
BF16 = jnp.bfloat16
HIGH = lax.Precision.HIGHEST

NX, NY, NZ = 4, 8, 16
Q = 4
ROWS = 80
DEC = 64
PAD = 96
HALF = ROWS // 2
CUT = 48
PART = PAD // 4
SLOT = 16
USED = 10
CAP = 160


def adamw(g, m, v, p, inv_one, inv_two):
    m = beta_one * m + (1.0 - beta_one) * g
    v = beta_two * v + (1.0 - beta_two) * g * g
    p = p - learn_rate * (m * inv_one / (jnp.sqrt(v * inv_two) + epsilon) + weight_decay * p)
    return m, v, p


def kernel(
    step_ref,
    own_ref,
    dec_grad,
    vis_grad,
    dec_p,
    dec_m,
    dec_v,
    vis_p,
    vis_m,
    vis_v,
    n_dec,
    n_vis,
    w_dec,
    w_vis,
    a_dec,
    b_dec,
    a_vis,
    b_vis,
    s_dec,
    s_vis,
    acc,
    ry,
    ay,
    rx,
    ak,
    rx2,
    ry2,
    ax,
    rz,
    az,
    ryh,
    ah,
    rzh,
    tz,
    g4,
    gdec,
    wall,
    st,
    stm,
    stx,
    gx,
    gm,
    gr,
    owner,
    lsem,
    ssem,
    rsem,
):
    rep, sh = lax.axis_index("replica"), lax.axis_index("shard")
    core = lax.rem(rep, 2)
    z = lax.rem(rep // 2, NZ)
    yl = lax.rem(sh, Q)
    y = (rep // (2 * NZ)) * Q + yl
    x = sh // Q
    zq = lax.rem(z, 4)

    def dev(dx=0, dy=0, dz=0, dc=0):
        xx = lax.rem(x + dx + NX, NX)
        yy = lax.rem(y + dy + NY, NY)
        zz = lax.rem(z + dz + NZ, NZ)
        cc = lax.rem(core + dc, 2)
        return ((yy // Q) * NZ + zz) * 2 + cc, xx * Q + lax.rem(yy, Q)

    def at4(i, d):
        return lax.rem(i + d + 4, 4)

    used = [0]

    def remote(src, dst, target):
        k = used[0]
        used[0] += 1
        return pltpu.make_async_remote_copy(
            src_ref=src,
            dst_ref=dst,
            send_sem=ssem.at[k],
            recv_sem=rsem.at[k],
            device_id=target,
            device_id_type=MESH,
        )

    locals_used = [0]

    def local(src, dst):
        k = locals_used[0]
        locals_used[0] += 1
        return pltpu.make_async_copy(src, dst, lsem.at[k])

    def go(copies):
        for c in copies:
            c.start()

    def done(copies):
        for c in copies:
            c.wait()

    is_dec, is_vis = core == 0, core == 1

    load_dec = local(dec_grad.at[0], a_dec)
    load_vis = local(vis_grad.at[0], a_vis)
    load_maps = [local(own_ref, owner)]
    load_state = [
        local(src, dst)
        for src, dst in (
            (dec_p, s_dec.at[0]),
            (dec_m, s_dec.at[1]),
            (dec_v, s_dec.at[2]),
            (vis_p, s_vis.at[0]),
            (vis_m, s_vis.at[1]),
            (vis_v, s_vis.at[2]),
        )
    ]

    @pl.when(is_dec)
    def _():
        load_dec.start()

    @pl.when(is_vis)
    def _():
        load_vis.start()

    go(load_maps)
    go(load_state)

    friends = [dev(dc=1)]
    friends += [dev(dx=d) for d in (1, -1, 2)]
    friends += [dev(dy=d) for d in (1, -1, 2, -2, 4)]
    friends += [dev(dz=d) for d in (1, -1, 2, -2, 4, -4, 8)]
    barrier = pltpu.get_barrier_semaphore()
    for friend in friends:
        pl.semaphore_signal(barrier, inc=1, device_id=friend, device_id_type=MESH)
    pl.semaphore_wait(barrier, len(friends))

    send_vis = remote(vis_grad.at[0], b_vis, dev(dc=1))
    send_dec = remote(dec_grad.at[0], b_dec, dev(dc=1))

    @pl.when(is_dec)
    def _():
        send_vis.start()
        load_dec.wait()
        send_dec.wait_recv()

        @pl.loop(0, DEC)
        def _(j):
            at = pl.multiple_of(j * 128, 128)
            block = a_dec[:, pl.ds(at, 128)].astype(F32) + b_dec[:, pl.ds(at, 128)].astype(F32)
            acc.reshape(16 * ROWS, 128)[pl.ds(j, 16, stride=ROWS), :] = block

        for i in range(16):
            acc[i // 4, i % 4, DEC:ROWS, :] = jnp.zeros((ROWS - DEC, 128), F32)
        send_vis.wait_send()

    @pl.when(is_vis)
    def _():
        send_dec.start()
        load_vis.wait()
        send_vis.wait_recv()

        for i in range(16):
            part = pl.ds(i * ROWS, ROWS)
            acc[i // 4, i % 4] = a_vis[part, :].astype(F32) + b_vis[part, :].astype(F32)
        send_dec.wait_send()

    q1, q2, q3 = at4(yl, 1), at4(yl, 2), at4(yl, 3)
    x1, x2, x3 = at4(x, 1), at4(x, 2), at4(x, 3)
    lo, hi = pl.ds(0, 2), pl.ds(2, 2)
    one, two = pl.ds(0, HALF), pl.ds(HALF, HALF)
    first_y = [
        remote(acc.at[lo, q2, one], ry.at[2, lo], dev(dy=2)),
        remote(acc.at[hi, q2, one], ry.at[2, hi], dev(dy=-2)),
        remote(acc.at[:, q1, one], ry.at[0], dev(dy=1)),
        remote(acc.at[:, q3, one], ry.at[1], dev(dy=-1)),
    ]
    first_x = [
        remote(acc.at[x2, :, two], rx.at[2], dev(dx=2)),
        remote(acc.at[x1, :, two], rx.at[0], dev(dx=1)),
        remote(acc.at[x3, :, two], rx.at[1], dev(dx=-1)),
    ]
    for a, b in itertools.zip_longest(first_y, first_x):
        a.start()
        if b is not None:
            b.start()
    second_x = [
        remote(ay.at[x2], rx2.at[2], dev(dx=2)),
        remote(ay.at[x1], rx2.at[0], dev(dx=1)),
        remote(ay.at[x3], rx2.at[1], dev(dx=-1)),
    ]
    second_y = [
        remote(ak.at[q2], ry2.at[2], dev(dy=2)),
        remote(ak.at[q1], ry2.at[0], dev(dy=1)),
        remote(ak.at[q3], ry2.at[1], dev(dy=-1)),
    ]
    done(first_y)
    for i in range(NX):
        ay[i] = (acc[i, yl, one, :] + ry[0, i]) + (ry[1, i] + ry[2, i])
    go(second_x)
    done(first_x)
    for i in range(Q):
        ak[i] = (acc[x, i, two, :] + rx[0, i]) + (rx[1, i] + rx[2, i])
    go(second_y)
    done(second_x)
    ax[0:HALF, :] = (ay[x] + rx2[0]) + (rx2[1] + rx2[2])
    done(second_y)
    ax[HALF:ROWS, :] = (ak[yl] + ry2[0]) + (ry2[1] + ry2[2])
    ax[ROWS:PAD, :] = jnp.zeros((PAD - ROWS, 128), F32)

    def part_of(i):
        return pl.ds(pl.multiple_of(i * PART, 8), PART)

    copies = [
        remote(ax.at[part_of(at4(zq, 2))], rz.at[2], dev(dz=2)),
        remote(ax.at[part_of(at4(zq, 1))], rz.at[0], dev(dz=1)),
        remote(ax.at[part_of(at4(zq, 3))], rz.at[1], dev(dz=-1)),
    ]
    go(copies)

    done(load_state)
    for i in range(16):
        for k in range(3):
            st[i, k * SLOT : k * SLOT + SLOT, :] = jnp.zeros((SLOT, 128), F32)
            st[i, k * SLOT : k * SLOT + USED, :] = s_vis[k, i * USED : i * USED + USED, :]

    def along_x(src, dst):
        return [
            remote(src.at[pl.ds(at4(x, d) * 4, 4)], dst.at[x], dev(dx=e))
            for d, e in ((2, 2), (1, 1), (3, -1))
        ]

    def along_y(src, dst):
        return [
            remote(src.at[:, at4(yl, d)], dst.at[:, yl], dev(dy=e))
            for d, e in ((2, 2), (1, 1), (3, -1))
        ]

    st_x = along_x(st, stm)
    st_y = along_y(stm, stx)
    back = [at4(x, d) for d in (-2, -1, 1)]

    @pl.when(is_vis)
    def _():
        go(st_x)
        stm[x] = st[pl.ds(x * 4, 4)]

    done(copies)
    az[...] = (ax[part_of(zq), :] + rz[0]) + (rz[1] + rz[2])

    far = remote(az, ryh, dev(dy=4))
    far.start()

    @pl.when(is_vis)
    def _():
        done(st_x)

    far.wait()
    ah[...] = az[...] + ryh[...]
    copies = [
        remote(ah, rzh.at[2], dev(dz=8)),
        remote(ah, rzh.at[0], dev(dz=4)),
        remote(ah, rzh.at[1], dev(dz=-4)),
    ]
    go(copies)

    @pl.when(is_vis)
    def _():
        go(st_y)
        stx[:, yl] = stm[:, yl]

    done(load_maps)
    t = jnp.full((1, 128), step_ref[0].astype(F32), F32)
    inv_one = 1.0 / (1.0 - jnp.exp(t * math.log(beta_one)))
    inv_two = 1.0 / (1.0 - jnp.exp(t * math.log(beta_two)))

    lane = lax.broadcasted_iota(jnp.int32, (1, ROWS), 1)
    own = lax.fori_loop(
        0,
        ROWS,
        lambda i, v: jnp.where(lane == i, owner[sh * ROWS + i], v),
        jnp.zeros((1, ROWS), jnp.int32),
    )
    one_hot = (lax.broadcasted_iota(jnp.int32, (16, ROWS), 0) == own).astype(F32)
    before = (
        lax.broadcasted_iota(jnp.int32, (ROWS, ROWS), 0)
        < lax.broadcasted_iota(jnp.int32, (ROWS, ROWS), 1)
    ).astype(F32)
    count = jnp.dot(one_hot, before, preferred_element_type=F32)
    position = jnp.sum(one_hot * count, axis=0, keepdims=True)
    key = own * SLOT + position.astype(jnp.int32)
    pick = (lax.broadcasted_iota(jnp.int32, (16 * SLOT, ROWS), 0) == key).astype(F32)

    def blocks_of(k):
        rows = stx[:, :, k * SLOT : k * SLOT + SLOT, :].reshape(16 * SLOT, 128)
        return lax.dot_general(
            pick, rows, (((0,), (0,)), ((), ())), precision=HIGH, preferred_element_type=F32
        )

    @pl.when(is_vis)
    def _():
        done(st_y)
        for k in range(3):
            n_vis[k, 0:ROWS, :] = blocks_of(k)

    done(copies)
    tz[...] = (ah[...] + rzh[2]) + (rzh[0] + rzh[1])

    copies = [
        remote(tz, g4.at[zq], dev(dz=2)),
        remote(tz, g4.at[zq], dev(dz=1)),
        remote(tz, g4.at[zq], dev(dz=-1)),
    ]
    go(copies)
    g4[zq] = tz[...]
    done(copies)

    g_x = along_x(gx, gm)
    g_y = along_y(gm, gr)
    dec_over = remote(gdec, gdec, dev(dc=1))
    vis_over = remote(gr, gr, dev(dc=1))

    @pl.when(is_dec)
    def _():
        g = g4[...].reshape(PAD, 128)[0:DEC]
        gdec[...] = g
        dec_over.start()
        _, _, p = adamw(g, s_dec[1], s_dec[2], s_dec[0], inv_one, inv_two)
        wall[x, yl, 0:DEC, :] = p.astype(BF16)
        wall[x, yl, DEC:ROWS, :] = jnp.zeros((ROWS - DEC, 128), BF16)

    @pl.when(is_vis)
    def _():
        g = g4[...].reshape(PAD, 128)[0:ROWS]
        _, _, p = adamw(
            g, n_vis[1, 0:ROWS, :], n_vis[2, 0:ROWS, :], n_vis[0, 0:ROWS, :], inv_one, inv_two
        )
        wall[x, yl] = p.astype(BF16)

    up, down = pl.ds(0, CUT), pl.ds(CUT, ROWS - CUT)

    def weights(view, device):
        return remote(view, view, device)

    w_x = [weights(wall.at[x, yl, up], dev(dx=d)) for d in (2, 1, -1)]
    w_y = [weights(wall.at[x, yl, down], dev(dy=d)) for d in (2, 1, -1)]
    go(w_x)
    go(w_y)

    @pl.when(is_vis)
    def _():
        g = g4[...].reshape(PAD, 128)[0:ROWS]
        rows = jnp.dot(pick, g, precision=HIGH, preferred_element_type=F32)
        gx[...] = rows.reshape(16, SLOT, 128)
        go(g_x)
        gm[x] = gx[pl.ds(x * 4, 4)]

    w_xy = [
        weights(wall.at[lo, yl, up], dev(dy=2)),
        weights(wall.at[hi, yl, up], dev(dy=-2)),
        weights(wall.at[:, yl, up], dev(dy=1)),
        weights(wall.at[:, yl, up], dev(dy=-1)),
    ]
    w_yx = [weights(wall.at[x, :, down], dev(dx=d)) for d in (2, 1, -1)]
    done(w_x)
    go(w_xy)
    done(w_y)
    go(w_yx)

    @pl.when(is_vis)
    def _():
        done(g_x)
        go(g_y)
        gr[:, yl] = gm[:, yl]
        dec_over.wait_recv()

    m, v, p = adamw(gdec[...], s_dec[1], s_dec[2], s_dec[0], inv_one, inv_two)
    n_dec[0], n_dec[1], n_dec[2] = p, m, v

    @pl.when(is_vis)
    def _():
        done(g_y)
        vis_over.start()

    @pl.when(is_dec)
    def _():
        vis_over.wait_recv()

    for i in range(16):
        part = pl.ds(i * USED, USED)
        g = gr[i // 4, i % 4, 0:USED, :]
        m, v, p = adamw(
            g, s_vis[1, part, :], s_vis[2, part, :], s_vis[0, part, :], inv_one, inv_two
        )
        n_vis[0, part, :] = p
        n_vis[1, part, :] = m
        n_vis[2, part, :] = v
    done(w_xy)
    done(w_yx)

    over_v = remote(wall, w_vis, dev(dc=1))
    over_d = remote(wall, w_dec, dev(dc=1))

    @pl.when(is_vis)
    def _():
        over_v.start()
        w_vis[...] = wall[...]
        over_d.wait_recv()
        over_v.wait_send()
        vis_over.wait_send()

    @pl.when(is_dec)
    def _():
        over_d.start()
        w_dec[...] = wall[...]
        over_v.wait_recv()
        over_d.wait_send()
        dec_over.wait_send()


def finish(
    n_dec, n_vis, w_dec, w_vis, o_dp, o_dm, o_dv, o_dw, o_vp, o_vm, o_vv, o_vw, wide, dw, sems
):
    pairs = [(n_dec.at[k], o) for k, o in enumerate((o_dp, o_dm, o_dv))]
    pairs += [(n_vis.at[k], o) for k, o in enumerate((o_vp, o_vm, o_vv))]
    pairs.append((w_vis.reshape(16 * ROWS, 128), o_vw))
    copies = [pltpu.make_async_copy(a, b, sems.at[k]) for k, (a, b) in enumerate(pairs)]
    for c in copies:
        c.start()
    for i in range(16):
        wide[i * DEC : i * DEC + DEC, :] = w_dec[i // 4, i % 4, 0:DEC, :].astype(F32)
    for j in range(DEC):
        dw[:, j * 128 : j * 128 + 128] = wide[pl.ds(j, 16, stride=DEC), :].astype(BF16)
    last = pltpu.make_async_copy(dw, o_dw, sems.at[len(pairs)])
    last.start()
    for c in copies:
        c.wait()
    last.wait()


def body(
    dec_grad,
    dec_master,
    dec_moment,
    dec_second,
    vis_grad,
    vis_owner,
    vis_master,
    vis_moment,
    vis_second,
    step_count,
):
    anywhere = pl.BlockSpec(memory_space=pl.ANY)
    sds = jax.ShapeDtypeStruct
    vmem = pltpu.VMEM
    inner_shape = [
        vmem((3, DEC, 128), F32),
        vmem((3, CAP, 128), F32),
        vmem((4, 4, ROWS, 128), BF16),
        vmem((4, 4, ROWS, 128), BF16),
    ]
    out_shape = [
        sds((DEC, 128), F32),
        sds((DEC, 128), F32),
        sds((DEC, 128), F32),
        sds((16, DEC * 128), BF16),
        sds((CAP, 128), F32),
        sds((CAP, 128), F32),
        sds((CAP, 128), F32),
        sds((16 * ROWS, 128), BF16),
    ]
    on_chip = pl.BlockSpec(memory_space=pltpu.VMEM)
    scratch = [
        vmem((16, DEC * 128), BF16),
        vmem((16, DEC * 128), BF16),
        vmem((16 * ROWS, 128), BF16),
        vmem((16 * ROWS, 128), BF16),
        vmem((3, DEC, 128), F32),
        vmem((3, CAP, 128), F32),
        vmem((4, 4, ROWS, 128), F32),
        vmem((3, 4, HALF, 128), F32),
        vmem((4, HALF, 128), F32),
        vmem((3, 4, HALF, 128), F32),
        vmem((4, HALF, 128), F32),
        vmem((3, HALF, 128), F32),
        vmem((3, HALF, 128), F32),
        vmem((PAD, 128), F32),
        vmem((3, PART, 128), F32),
        vmem((PART, 128), F32),
        vmem((PART, 128), F32),
        vmem((PART, 128), F32),
        vmem((3, PART, 128), F32),
        vmem((PART, 128), F32),
        vmem((4, PART, 128), F32),
        vmem((DEC, 128), F32),
        vmem((4, 4, ROWS, 128), BF16),
        vmem((16, 3 * SLOT, 128), F32),
        vmem((4, 4, 3 * SLOT, 128), F32),
        vmem((4, 4, 3 * SLOT, 128), F32),
        vmem((16, SLOT, 128), F32),
        vmem((4, 4, SLOT, 128), F32),
        vmem((4, 4, SLOT, 128), F32),
        pltpu.SMEM((16 * ROWS,), jnp.int32),
        pltpu.SemaphoreType.DMA((20,)),
        pltpu.SemaphoreType.DMA((64,)),
        pltpu.SemaphoreType.DMA((64,)),
    ]
    inner = pl.pallas_call(
        kernel,
        out_shape=inner_shape,
        in_specs=[pl.BlockSpec(memory_space=pltpu.SMEM)]
        + [pl.BlockSpec(memory_space=pltpu.HBM)] * 9,
        out_specs=[on_chip] * 4,
        scratch_shapes=scratch,
        compiler_params=pltpu.CompilerParams(collective_id=0, has_side_effects=True),
    )(
        step_count,
        vis_owner,
        dec_grad,
        vis_grad,
        dec_master.reshape(DEC, 128),
        dec_moment.reshape(DEC, 128),
        dec_second.reshape(DEC, 128),
        vis_master,
        vis_moment,
        vis_second,
    )
    outs = pl.pallas_call(
        finish,
        out_shape=out_shape,
        in_specs=[on_chip] * 4,
        out_specs=[anywhere] * 8,
        scratch_shapes=[
            vmem((16 * DEC, 128), F32),
            vmem((16, DEC * 128), BF16),
            pltpu.SemaphoreType.DMA((8,)),
        ],
    )(*[pltpu.with_memory_space_constraint(a, pltpu.VMEM) for a in inner])
    outs = list(outs)
    for i in range(3):
        outs[i] = outs[i].reshape(1, DEC * 128)
    return tuple(outs)


def solution(mesh):
    in_specs = (
        P(("replica", "shard"), None, None),
        P("shard", None),
        P("shard", None),
        P("shard", None),
        P(("replica", "shard"), None, None),
        P(),
        P("shard", None),
        P("shard", None),
        P("shard", None),
        P(),
    )
    out_specs = (
        P("shard", None),
        P("shard", None),
        P("shard", None),
        P(),
        P("shard", None),
        P("shard", None),
        P("shard", None),
        P(),
    )
    return jax.shard_map(body, mesh=mesh, in_specs=in_specs, out_specs=out_specs, check_vma=False)
```

```python
import itertools
import math

import jax
import jax.numpy as jnp
from jax import lax
from jax.experimental import pallas as pl
from jax.experimental.pallas import tpu as pltpu
from jax.sharding import PartitionSpec as P

beta_one = 0.9
beta_two = 0.999
learn_rate = 0.02
weight_decay = 0.1
epsilon = 1e-08

MESH = pl.DeviceIdType.MESH
F32 = jnp.float32
BF16 = jnp.bfloat16
HIGH = lax.Precision.HIGHEST

NX, NY, NZ = 4, 8, 16
Q = 4
ROWS = 80
DEC = 64
PAD = 96
HALF = ROWS // 2
CUT = 48
PART = PAD // 4
SLOT = 16
USED = 10
CAP = 160


def adamw(g, m, v, p, inv_one, inv_two):
    m = beta_one * m + (1.0 - beta_one) * g
    v = beta_two * v + (1.0 - beta_two) * g * g
    p = p - learn_rate * (m * inv_one / (jnp.sqrt(v * inv_two) + epsilon) + weight_decay * p)
    return m, v, p


def kernel(
    step_ref,
    own_ref,
    dec_grad,
    vis_grad,
    dec_p,
    dec_m,
    dec_v,
    vis_p,
    vis_m,
    vis_v,
    n_dec,
    n_vis,
    wall,
    other,
    a_dec,
    b_dec,
    a_vis,
    b_vis,
    s_dec,
    s_vis,
    acc,
    ry,
    ay,
    rx,
    ak,
    rx2,
    ry2,
    ax,
    rz,
    az,
    ryh,
    ah,
    rzh,
    tz,
    g4,
    gdec,
    st,
    stm,
    stx,
    gx,
    gm,
    gr,
    owner,
    lsem,
    ssem,
    rsem,
    near_sem,
    far_sem,
):
    rep, sh = lax.axis_index("replica"), lax.axis_index("shard")
    core = lax.rem(rep, 2)
    z = lax.rem(rep // 2, NZ)
    yl = lax.rem(sh, Q)
    y = (rep // (2 * NZ)) * Q + yl
    x = sh // Q
    zq = lax.rem(z, 4)

    def dev(dx=0, dy=0, dz=0, dc=0):
        xx = lax.rem(x + dx + NX, NX)
        yy = lax.rem(y + dy + NY, NY)
        zz = lax.rem(z + dz + NZ, NZ)
        cc = lax.rem(core + dc, 2)
        return ((yy // Q) * NZ + zz) * 2 + cc, xx * Q + lax.rem(yy, Q)

    def at4(i, d):
        return lax.rem(i + d + 4, 4)

    used = [0]

    def remote(src, dst, target):
        k = used[0]
        used[0] += 1
        return pltpu.make_async_remote_copy(
            src_ref=src,
            dst_ref=dst,
            send_sem=ssem.at[k],
            recv_sem=rsem.at[k],
            device_id=target,
            device_id_type=MESH,
        )

    locals_used = [0]

    def local(src, dst):
        k = locals_used[0]
        locals_used[0] += 1
        return pltpu.make_async_copy(src, dst, lsem.at[k])

    def go(copies):
        for c in copies:
            c.start()

    def done(copies):
        for c in copies:
            c.wait()

    is_dec, is_vis = core == 0, core == 1

    load_dec = local(dec_grad.at[0], a_dec)
    load_vis = local(vis_grad.at[0], a_vis)
    load_maps = [local(own_ref, owner)]
    load_state = [
        local(src, dst)
        for src, dst in (
            (dec_p, s_dec.at[0]),
            (dec_m, s_dec.at[1]),
            (dec_v, s_dec.at[2]),
            (vis_p, s_vis.at[0]),
            (vis_m, s_vis.at[1]),
            (vis_v, s_vis.at[2]),
        )
    ]

    @pl.when(is_dec)
    def _():
        load_dec.start()

    @pl.when(is_vis)
    def _():
        load_vis.start()

    go(load_maps)
    go(load_state)

    friends = [dev(dc=1)]
    friends += [dev(dx=d) for d in (1, -1, 2)]
    friends += [dev(dy=d) for d in (1, -1, 2, -2)]
    friends += [dev(dz=d) for d in (1, -1, 2, -2)]
    barrier = pltpu.get_barrier_semaphore()
    for friend in friends:
        pl.semaphore_signal(barrier, inc=1, device_id=friend, device_id_type=MESH)
    pl.semaphore_wait(barrier, len(friends))

    for d in (2, -2):
        pl.semaphore_signal(near_sem, inc=1, device_id=dev(dz=d), device_id_type=MESH)

    send_vis = remote(vis_grad.at[0], b_vis, dev(dc=1))
    send_dec = remote(dec_grad.at[0], b_dec, dev(dc=1))

    @pl.when(is_dec)
    def _():
        send_vis.start()
        load_dec.wait()
        send_dec.wait_recv()

        @pl.loop(0, DEC)
        def _(j):
            at = pl.multiple_of(j * 128, 128)
            block = a_dec[:, pl.ds(at, 128)].astype(F32) + b_dec[:, pl.ds(at, 128)].astype(F32)
            acc.reshape(16 * ROWS, 128)[pl.ds(j, 16, stride=ROWS), :] = block

        for i in range(16):
            acc[i // 4, i % 4, DEC:ROWS, :] = jnp.zeros((ROWS - DEC, 128), F32)
        send_vis.wait_send()

    @pl.when(is_vis)
    def _():
        send_dec.start()
        load_vis.wait()
        send_vis.wait_recv()

        for i in range(16):
            part = pl.ds(i * ROWS, ROWS)
            acc[i // 4, i % 4] = a_vis[part, :].astype(F32) + b_vis[part, :].astype(F32)
        send_dec.wait_send()

    q1, q2, q3 = at4(yl, 1), at4(yl, 2), at4(yl, 3)
    x1, x2, x3 = at4(x, 1), at4(x, 2), at4(x, 3)
    lo, hi = pl.ds(0, 2), pl.ds(2, 2)
    one, two = pl.ds(0, HALF), pl.ds(HALF, HALF)
    first_y = [
        remote(acc.at[lo, q2, one], ry.at[2, lo], dev(dy=2)),
        remote(acc.at[hi, q2, one], ry.at[2, hi], dev(dy=-2)),
        remote(acc.at[:, q1, one], ry.at[0], dev(dy=1)),
        remote(acc.at[:, q3, one], ry.at[1], dev(dy=-1)),
    ]
    first_x = [
        remote(acc.at[x2, :, two], rx.at[2], dev(dx=2)),
        remote(acc.at[x1, :, two], rx.at[0], dev(dx=1)),
        remote(acc.at[x3, :, two], rx.at[1], dev(dx=-1)),
    ]
    for a, b in itertools.zip_longest(first_y, first_x):
        a.start()
        if b is not None:
            b.start()
    second_x = [
        remote(ay.at[x2], rx2.at[2], dev(dx=2)),
        remote(ay.at[x1], rx2.at[0], dev(dx=1)),
        remote(ay.at[x3], rx2.at[1], dev(dx=-1)),
    ]
    second_y = [
        remote(ak.at[q2], ry2.at[2], dev(dy=2)),
        remote(ak.at[q1], ry2.at[0], dev(dy=1)),
        remote(ak.at[q3], ry2.at[1], dev(dy=-1)),
    ]
    pl.semaphore_wait(near_sem, 2)
    for d in (4, -4):
        pl.semaphore_signal(far_sem, inc=1, device_id=dev(dz=d), device_id_type=MESH)
    done(first_y)
    for i in range(NX):
        ay[i] = (acc[i, yl, one, :] + ry[0, i]) + (ry[1, i] + ry[2, i])
    go(second_x)
    done(first_x)
    for i in range(Q):
        ak[i] = (acc[x, i, two, :] + rx[0, i]) + (rx[1, i] + rx[2, i])
    go(second_y)
    done(second_x)
    ax[0:HALF, :] = (ay[x] + rx2[0]) + (rx2[1] + rx2[2])
    done(second_y)
    ax[HALF:ROWS, :] = (ak[yl] + ry2[0]) + (ry2[1] + ry2[2])
    ax[ROWS:PAD, :] = jnp.zeros((PAD - ROWS, 128), F32)

    def part_of(i):
        return pl.ds(pl.multiple_of(i * PART, 8), PART)

    copies = [
        remote(ax.at[part_of(at4(zq, 2))], rz.at[2], dev(dz=2)),
        remote(ax.at[part_of(at4(zq, 1))], rz.at[0], dev(dz=1)),
        remote(ax.at[part_of(at4(zq, 3))], rz.at[1], dev(dz=-1)),
    ]
    go(copies)

    done(load_state)
    for i in range(16):
        for k in range(3):
            st[i, k * SLOT : k * SLOT + SLOT, :] = jnp.zeros((SLOT, 128), F32)
            st[i, k * SLOT : k * SLOT + USED, :] = s_vis[k, i * USED : i * USED + USED, :]

    def along_x(src, dst):
        return [
            remote(src.at[pl.ds(at4(x, d) * 4, 4)], dst.at[x], dev(dx=e))
            for d, e in ((2, 2), (1, 1), (3, -1))
        ]

    def along_y(src, dst):
        return [
            remote(src.at[:, at4(yl, d)], dst.at[:, yl], dev(dy=e))
            for d, e in ((2, 2), (1, 1), (3, -1))
        ]

    st_x = along_x(st, stm)
    st_y = along_y(stm, stx)

    @pl.when(is_vis)
    def _():
        go(st_x)
        stm[x] = st[pl.ds(x * 4, 4)]

    done(copies)
    az[...] = (ax[part_of(zq), :] + rz[0]) + (rz[1] + rz[2])

    ra, rb = pl.ds(0, 16), pl.ds(16, PART - 16)

    def along_far_z(src, rows):
        return [
            remote(src.at[rows], rzh.at[2, rows], dev(dz=8)),
            remote(src.at[rows], rzh.at[0, rows], dev(dz=4)),
            remote(src.at[rows], rzh.at[1, rows], dev(dz=-4)),
        ]

    def far_sum(own, rows):
        return (own[rows, :] + rzh[2, rows, :]) + (rzh[0, rows, :] + rzh[1, rows, :])

    far_a = remote(az.at[ra], ryh.at[ra], dev(dy=4))
    far_a.start()
    pl.semaphore_wait(far_sem, 2)
    z_b = along_far_z(az, rb)
    go(z_b)

    @pl.when(is_vis)
    def _():
        done(st_x)

    far_a.wait()
    ah[ra, :] = az[ra, :] + ryh[ra, :]
    z_a = along_far_z(ah, ra)
    go(z_a)

    @pl.when(is_vis)
    def _():
        go(st_y)
        stx[:, yl] = stm[:, yl]

    done(z_b)
    ah[rb, :] = far_sum(az, rb)
    far_b = remote(ah.at[rb], ryh.at[rb], dev(dy=4))
    far_b.start()

    done(load_maps)
    t = jnp.full((1, 128), step_ref[0].astype(F32), F32)
    inv_one = 1.0 / (1.0 - jnp.exp(t * math.log(beta_one)))
    inv_two = 1.0 / (1.0 - jnp.exp(t * math.log(beta_two)))

    lane = lax.broadcasted_iota(jnp.int32, (1, ROWS), 1)
    own = lax.fori_loop(
        0,
        ROWS,
        lambda i, v: jnp.where(lane == i, owner[sh * ROWS + i], v),
        jnp.zeros((1, ROWS), jnp.int32),
    )
    one_hot = (lax.broadcasted_iota(jnp.int32, (16, ROWS), 0) == own).astype(F32)
    before = (
        lax.broadcasted_iota(jnp.int32, (ROWS, ROWS), 0)
        < lax.broadcasted_iota(jnp.int32, (ROWS, ROWS), 1)
    ).astype(F32)
    count = jnp.dot(one_hot, before, preferred_element_type=F32)
    position = jnp.sum(one_hot * count, axis=0, keepdims=True)
    key = own * SLOT + position.astype(jnp.int32)
    pick = (lax.broadcasted_iota(jnp.int32, (16 * SLOT, ROWS), 0) == key).astype(F32)

    def blocks_of(k):
        rows = stx[:, :, k * SLOT : k * SLOT + SLOT, :].reshape(16 * SLOT, 128)
        return lax.dot_general(
            pick, rows, (((0,), (0,)), ((), ())), precision=HIGH, preferred_element_type=F32
        )

    @pl.when(is_vis)
    def _():
        done(st_y)
        for k in range(3):
            n_vis[k, 0:ROWS, :] = blocks_of(k)

    far_b.wait()
    tz[rb, :] = ah[rb, :] + ryh[rb, :]
    done(z_a)
    tz[ra, :] = far_sum(ah, ra)

    copies = [
        remote(tz, g4.at[zq], dev(dz=2)),
        remote(tz, g4.at[zq], dev(dz=1)),
        remote(tz, g4.at[zq], dev(dz=-1)),
    ]
    go(copies)
    g4[zq] = tz[...]
    done(copies)

    g_x = along_x(gx, gm)
    g_y = along_y(gm, gr)
    dec_over = remote(gdec, gdec, dev(dc=1))
    vis_over = remote(gr, gr, dev(dc=1))

    @pl.when(is_dec)
    def _():
        g = g4[...].reshape(PAD, 128)[0:DEC]
        gdec[...] = g
        dec_over.start()
        _, _, p = adamw(g, s_dec[1], s_dec[2], s_dec[0], inv_one, inv_two)
        wall[x, yl, 0:DEC, :] = p.astype(BF16)
        wall[x, yl, DEC:ROWS, :] = jnp.zeros((ROWS - DEC, 128), BF16)

    @pl.when(is_vis)
    def _():
        g = g4[...].reshape(PAD, 128)[0:ROWS]
        _, _, p = adamw(
            g, n_vis[1, 0:ROWS, :], n_vis[2, 0:ROWS, :], n_vis[0, 0:ROWS, :], inv_one, inv_two
        )
        wall[x, yl] = p.astype(BF16)

    up, down = pl.ds(0, CUT), pl.ds(CUT, ROWS - CUT)

    def weights(view, device):
        return remote(view, view, device)

    w_x = [weights(wall.at[x, yl, up], dev(dx=d)) for d in (2, 1, -1)]
    w_y = [weights(wall.at[x, yl, down], dev(dy=d)) for d in (2, 1, -1)]
    go(w_x)
    go(w_y)

    @pl.when(is_vis)
    def _():
        g = g4[...].reshape(PAD, 128)[0:ROWS]
        rows = jnp.dot(pick, g, precision=HIGH, preferred_element_type=F32)
        gx[...] = rows.reshape(16, SLOT, 128)
        go(g_x)
        gm[x] = gx[pl.ds(x * 4, 4)]

    w_xy = [
        weights(wall.at[:, yl, up], dev(dy=1)),
        weights(wall.at[:, yl, up], dev(dy=-1)),
        weights(wall.at[lo, yl, up], dev(dy=2)),
        weights(wall.at[hi, yl, up], dev(dy=-2)),
    ]
    w_yx = [weights(wall.at[x, :, down], dev(dx=d)) for d in (1, -1, 2)]
    over = []

    def forward(*index):
        over.append(remote(wall.at[index], other.at[index], dev(dc=1)))
        over[-1].start()

    every = pl.ds(0, 4)
    done(w_x)
    go(w_xy)
    forward(every, yl, up)
    done(w_y)
    go(w_yx)
    forward(x, every, down)

    @pl.when(is_vis)
    def _():
        done(g_x)
        go(g_y)
        gr[:, yl] = gm[:, yl]
        dec_over.wait_recv()

    m, v, p = adamw(gdec[...], s_dec[1], s_dec[2], s_dec[0], inv_one, inv_two)
    n_dec[0], n_dec[1], n_dec[2] = p, m, v

    @pl.when(is_vis)
    def _():
        done(g_y)
        vis_over.start()

    w_xy[0].wait()
    forward(every, q3, up)
    w_yx[0].wait()
    forward(x3, every, down)
    w_xy[1].wait()
    forward(every, q1, up)
    w_yx[1].wait()
    forward(x1, every, down)
    w_xy[2].wait()
    forward(lo, q2, up)
    w_xy[3].wait()
    forward(hi, q2, up)
    w_yx[2].wait()
    forward(x2, every, down)

    @pl.when(is_dec)
    def _():
        vis_over.wait_recv()

    for i in range(16):
        part = pl.ds(i * USED, USED)
        g = gr[i // 4, i % 4, 0:USED, :]
        m, v, p = adamw(
            g, s_vis[1, part, :], s_vis[2, part, :], s_vis[0, part, :], inv_one, inv_two
        )
        n_vis[0, part, :] = p
        n_vis[1, part, :] = m
        n_vis[2, part, :] = v
    done(over)

    @pl.when(is_vis)
    def _():
        vis_over.wait_send()

    @pl.when(is_dec)
    def _():
        dec_over.wait_send()


def finish(
    n_dec, n_vis, mine, other, o_dp, o_dm, o_dv, o_dw, o_vp, o_vm, o_vv, o_vw, wide, dw, sems
):
    core = lax.rem(lax.axis_index("replica"), 2)
    pairs = [(n_dec.at[k], o) for k, o in enumerate((o_dp, o_dm, o_dv))]
    pairs += [(n_vis.at[k], o) for k, o in enumerate((o_vp, o_vm, o_vv))]
    copies = [pltpu.make_async_copy(a, b, sems.at[k]) for k, (a, b) in enumerate(pairs)]
    for c in copies:
        c.start()

    def weights(dec, vis):
        first = pltpu.make_async_copy(vis.reshape(16 * ROWS, 128), o_vw, sems.at[len(pairs)])
        first.start()
        for i in range(16):
            wide[i * DEC : i * DEC + DEC, :] = dec[i // 4, i % 4, 0:DEC, :].astype(F32)
        for j in range(DEC):
            dw[:, j * 128 : j * 128 + 128] = wide[pl.ds(j, 16, stride=DEC), :].astype(BF16)
        last = pltpu.make_async_copy(dw, o_dw, sems.at[len(pairs) + 1])
        last.start()
        first.wait()
        last.wait()

    @pl.when(core == 0)
    def _():
        weights(mine, other)

    @pl.when(core == 1)
    def _():
        weights(other, mine)

    for c in copies:
        c.wait()


def body(
    dec_grad,
    dec_master,
    dec_moment,
    dec_second,
    vis_grad,
    vis_owner,
    vis_master,
    vis_moment,
    vis_second,
    step_count,
):
    anywhere = pl.BlockSpec(memory_space=pl.ANY)
    sds = jax.ShapeDtypeStruct
    vmem = pltpu.VMEM
    inner_shape = [
        vmem((3, DEC, 128), F32),
        vmem((3, CAP, 128), F32),
        vmem((4, 4, ROWS, 128), BF16),
        vmem((4, 4, ROWS, 128), BF16),
    ]
    out_shape = [
        sds((DEC, 128), F32),
        sds((DEC, 128), F32),
        sds((DEC, 128), F32),
        sds((16, DEC * 128), BF16),
        sds((CAP, 128), F32),
        sds((CAP, 128), F32),
        sds((CAP, 128), F32),
        sds((16 * ROWS, 128), BF16),
    ]
    on_chip = pl.BlockSpec(memory_space=pltpu.VMEM)
    scratch = [
        vmem((16, DEC * 128), BF16),
        vmem((16, DEC * 128), BF16),
        vmem((16 * ROWS, 128), BF16),
        vmem((16 * ROWS, 128), BF16),
        vmem((3, DEC, 128), F32),
        vmem((3, CAP, 128), F32),
        vmem((4, 4, ROWS, 128), F32),
        vmem((3, 4, HALF, 128), F32),
        vmem((4, HALF, 128), F32),
        vmem((3, 4, HALF, 128), F32),
        vmem((4, HALF, 128), F32),
        vmem((3, HALF, 128), F32),
        vmem((3, HALF, 128), F32),
        vmem((PAD, 128), F32),
        vmem((3, PART, 128), F32),
        vmem((PART, 128), F32),
        vmem((PART, 128), F32),
        vmem((PART, 128), F32),
        vmem((3, PART, 128), F32),
        vmem((PART, 128), F32),
        vmem((4, PART, 128), F32),
        vmem((DEC, 128), F32),
        vmem((16, 3 * SLOT, 128), F32),
        vmem((4, 4, 3 * SLOT, 128), F32),
        vmem((4, 4, 3 * SLOT, 128), F32),
        vmem((16, SLOT, 128), F32),
        vmem((4, 4, SLOT, 128), F32),
        vmem((4, 4, SLOT, 128), F32),
        pltpu.SMEM((16 * ROWS,), jnp.int32),
        pltpu.SemaphoreType.DMA((20,)),
        pltpu.SemaphoreType.DMA((96,)),
        pltpu.SemaphoreType.DMA((96,)),
        pltpu.SemaphoreType.REGULAR,
        pltpu.SemaphoreType.REGULAR,
    ]
    inner = pl.pallas_call(
        kernel,
        out_shape=inner_shape,
        in_specs=[pl.BlockSpec(memory_space=pltpu.SMEM)]
        + [pl.BlockSpec(memory_space=pltpu.HBM)] * 9,
        out_specs=[on_chip] * 4,
        scratch_shapes=scratch,
        compiler_params=pltpu.CompilerParams(collective_id=0, has_side_effects=True),
    )(
        step_count,
        vis_owner,
        dec_grad,
        vis_grad,
        dec_master.reshape(DEC, 128),
        dec_moment.reshape(DEC, 128),
        dec_second.reshape(DEC, 128),
        vis_master,
        vis_moment,
        vis_second,
    )
    outs = pl.pallas_call(
        finish,
        out_shape=out_shape,
        in_specs=[on_chip] * 4,
        out_specs=[anywhere] * 8,
        scratch_shapes=[
            vmem((16 * DEC, 128), F32),
            vmem((16, DEC * 128), BF16),
            pltpu.SemaphoreType.DMA((8,)),
        ],
    )(*[pltpu.with_memory_space_constraint(a, pltpu.VMEM) for a in inner])
    outs = list(outs)
    for i in range(3):
        outs[i] = outs[i].reshape(1, DEC * 128)
    return tuple(outs)


def solution(mesh):
    in_specs = (
        P(("replica", "shard"), None, None),
        P("shard", None),
        P("shard", None),
        P("shard", None),
        P(("replica", "shard"), None, None),
        P(),
        P("shard", None),
        P("shard", None),
        P("shard", None),
        P(),
    )
    out_specs = (
        P("shard", None),
        P("shard", None),
        P("shard", None),
        P(),
        P("shard", None),
        P("shard", None),
        P("shard", None),
        P(),
    )
    return jax.shard_map(body, mesh=mesh, in_specs=in_specs, out_specs=out_specs, check_vma=False)
```

```python
import itertools
import math

import jax
import jax.numpy as jnp
from jax import lax
from jax.experimental import pallas as pl
from jax.experimental.pallas import tpu as pltpu
from jax.sharding import PartitionSpec as P

beta_one = 0.9
beta_two = 0.999
learn_rate = 0.02
weight_decay = 0.1
epsilon = 1e-08

MESH = pl.DeviceIdType.MESH
F32 = jnp.float32
BF16 = jnp.bfloat16
HIGH = lax.Precision.HIGHEST

NX, NY, NZ = 4, 8, 16
Q = 4
ROWS = 80
DEC = 64
PAD = 96
HALF = ROWS // 2
CUT = 48
PART = PAD // 4
SLOT = 16
USED = 10
CAP = 160
LOCALS, REMOTES = 9, 65
SENDS = 24


def adamw(g, m, v, p, inv_one, inv_two):
    m = beta_one * m + (1.0 - beta_one) * g
    v = beta_two * v + (1.0 - beta_two) * g * g
    p = p - learn_rate * (m * inv_one / (jnp.sqrt(v * inv_two) + epsilon) + weight_decay * p)
    return m, v, p


def kernel(
    step_ref,
    own_ref,
    dec_grad,
    vis_grad,
    dec_p,
    dec_m,
    dec_v,
    vis_p,
    vis_m,
    vis_v,
    n_dec,
    n_vis,
    wall,
    other,
    a_dec,
    b_dec,
    a_vis,
    b_vis,
    s_dec,
    s_vis,
    acc,
    ry,
    ay,
    rx,
    ak,
    rx2,
    ry2,
    ax,
    rz,
    az,
    ryh,
    ah,
    rzh,
    tz,
    g4,
    gdec,
    st,
    stm,
    stx,
    gx,
    gm,
    gr,
    owner,
    pick,
    lsem,
    ssem,
    rsem,
    near_sem,
    far_sem,
):
    rep, sh = lax.axis_index("replica"), lax.axis_index("shard")
    core = lax.rem(rep, 2)
    z = lax.rem(rep // 2, NZ)
    yl = lax.rem(sh, Q)
    y = (rep // (2 * NZ)) * Q + yl
    x = sh // Q
    zq = lax.rem(z, 4)

    def dev(dx=0, dy=0, dz=0, dc=0):
        xx = lax.rem(x + dx + NX, NX)
        yy = lax.rem(y + dy + NY, NY)
        zz = lax.rem(z + dz + NZ, NZ)
        cc = lax.rem(core + dc, 2)
        return ((yy // Q) * NZ + zz) * 2 + cc, xx * Q + lax.rem(yy, Q)

    def at4(i, d):
        return lax.rem(i + d + 4, 4)

    used = [0]

    def remote(src, dst, target):
        k = used[0]
        used[0] += 1
        return pltpu.make_async_remote_copy(
            src_ref=src,
            dst_ref=dst,
            send_sem=ssem.at[k % SENDS],
            recv_sem=rsem.at[k],
            device_id=target,
            device_id_type=MESH,
        )

    locals_used = [0]

    def local(src, dst):
        k = locals_used[0]
        locals_used[0] += 1
        return pltpu.make_async_copy(src, dst, lsem.at[k])

    def go(copies):
        for c in copies:
            c.start()

    def done(copies):
        for c in copies:
            c.wait()

    is_dec, is_vis = core == 0, core == 1

    load_dec = local(dec_grad.at[0], a_dec)
    load_vis = local(vis_grad.at[0], a_vis)
    load_maps = [local(own_ref, owner)]
    load_state = [
        local(src, dst)
        for src, dst in (
            (dec_p, s_dec.at[0]),
            (dec_m, s_dec.at[1]),
            (dec_v, s_dec.at[2]),
            (vis_p, s_vis.at[0]),
            (vis_m, s_vis.at[1]),
            (vis_v, s_vis.at[2]),
        )
    ]

    @pl.when(is_dec)
    def _():
        load_dec.start()

    @pl.when(is_vis)
    def _():
        load_vis.start()

    go(load_maps)
    go(load_state)

    friends = [dev(dc=1)]
    friends += [dev(dx=d) for d in (1, -1, 2)]
    friends += [dev(dy=d) for d in (1, -1, 2, -2)]
    friends += [dev(dz=d) for d in (1, -1, 2, -2)]
    barrier = pltpu.get_barrier_semaphore()
    for friend in friends:
        pl.semaphore_signal(barrier, inc=1, device_id=friend, device_id_type=MESH)
    pl.semaphore_wait(barrier, len(friends))

    for d in (2, -2):
        pl.semaphore_signal(near_sem, inc=1, device_id=dev(dz=d), device_id_type=MESH)

    send_vis = remote(vis_grad.at[0], b_vis, dev(dc=1))
    send_dec = remote(dec_grad.at[0], b_dec, dev(dc=1))

    @pl.when(is_dec)
    def _():
        send_vis.start()
        load_dec.wait()
        send_dec.wait_recv()

        @pl.loop(0, DEC)
        def _(j):
            at = pl.multiple_of(j * 128, 128)
            block = a_dec[:, pl.ds(at, 128)].astype(F32) + b_dec[:, pl.ds(at, 128)].astype(F32)
            acc.reshape(16 * ROWS, 128)[pl.ds(j, 16, stride=ROWS), :] = block

        send_vis.wait_send()

    @pl.when(is_vis)
    def _():
        send_dec.start()
        load_vis.wait()
        send_vis.wait_recv()

        for i in range(16):
            part = pl.ds(i * ROWS, ROWS)
            acc[i // 4, i % 4] = a_vis[part, :].astype(F32) + b_vis[part, :].astype(F32)
        send_dec.wait_send()

    def prepare():
        done(load_state)
        done(load_maps)
        for i in range(16):
            for k in range(3):
                st[i, k * SLOT : k * SLOT + SLOT, :] = jnp.zeros((SLOT, 128), F32)
                st[i, k * SLOT : k * SLOT + USED, :] = s_vis[k, i * USED : i * USED + USED, :]
        lane = lax.broadcasted_iota(jnp.int32, (1, ROWS), 1)
        own = lax.fori_loop(
            0,
            ROWS,
            lambda i, v: jnp.where(lane == i, owner[sh * ROWS + i], v),
            jnp.zeros((1, ROWS), jnp.int32),
        )
        one_hot = (lax.broadcasted_iota(jnp.int32, (16, ROWS), 0) == own).astype(F32)
        before = (
            lax.broadcasted_iota(jnp.int32, (ROWS, ROWS), 0)
            < lax.broadcasted_iota(jnp.int32, (ROWS, ROWS), 1)
        ).astype(F32)
        count = jnp.dot(one_hot, before, preferred_element_type=F32)
        position = jnp.sum(one_hot * count, axis=0, keepdims=True)
        key = own * SLOT + position.astype(jnp.int32)
        pick[...] = (lax.broadcasted_iota(jnp.int32, (16 * SLOT, ROWS), 0) == key).astype(F32)

    q1, q2, q3 = at4(yl, 1), at4(yl, 2), at4(yl, 3)
    x1, x2, x3 = at4(x, 1), at4(x, 2), at4(x, 3)
    lo, hi = pl.ds(0, 2), pl.ds(2, 2)

    def scatter(rows):
        half = rows // 2
        one, two, part = pl.ds(0, half), pl.ds(half, half), pl.ds(0, half)
        first_y = [
            remote(acc.at[lo, q2, one], ry.at[2, lo, part], dev(dy=2)),
            remote(acc.at[hi, q2, one], ry.at[2, hi, part], dev(dy=-2)),
            remote(acc.at[:, q1, one], ry.at[0, :, part], dev(dy=1)),
            remote(acc.at[:, q3, one], ry.at[1, :, part], dev(dy=-1)),
        ]
        first_x = [
            remote(acc.at[x2, :, two], rx.at[2, :, part], dev(dx=2)),
            remote(acc.at[x1, :, two], rx.at[0, :, part], dev(dx=1)),
            remote(acc.at[x3, :, two], rx.at[1, :, part], dev(dx=-1)),
        ]
        second_x = [
            remote(ay.at[x2, part], rx2.at[2, part], dev(dx=2)),
            remote(ay.at[x1, part], rx2.at[0, part], dev(dx=1)),
            remote(ay.at[x3, part], rx2.at[1, part], dev(dx=-1)),
        ]
        second_y = [
            remote(ak.at[q2, part], ry2.at[2, part], dev(dy=2)),
            remote(ak.at[q1, part], ry2.at[0, part], dev(dy=1)),
            remote(ak.at[q3, part], ry2.at[1, part], dev(dy=-1)),
        ]
        for a, b in itertools.zip_longest(first_y, first_x):
            a.start()
            if b is not None:
                b.start()
        pl.semaphore_wait(near_sem, 2)
        for d in (4, -4):
            pl.semaphore_signal(far_sem, inc=1, device_id=dev(dz=d), device_id_type=MESH)
        if rows == ROWS:
            prepare()
        else:
            done(load_state)
            done(load_maps)
        done(first_y)
        for i in range(NX):
            ay[i, part, :] = (acc[i, yl, one, :] + ry[0, i, part, :]) + (
                ry[1, i, part, :] + ry[2, i, part, :]
            )
        go(second_x)
        done(first_x)
        for i in range(Q):
            ak[i, part, :] = (acc[x, i, two, :] + rx[0, i, part, :]) + (
                rx[1, i, part, :] + rx[2, i, part, :]
            )
        go(second_y)
        done(second_x)
        ax[one, :] = (ay[x, part, :] + rx2[0, part, :]) + (rx2[1, part, :] + rx2[2, part, :])
        done(second_y)
        ax[two, :] = (ak[yl, part, :] + ry2[0, part, :]) + (ry2[1, part, :] + ry2[2, part, :])
        ax[rows:PAD, :] = jnp.zeros((PAD - rows, 128), F32)

    mark = used[0]

    @pl.when(is_dec)
    def _():
        scatter(DEC)

    used[0] = mark

    @pl.when(is_vis)
    def _():
        scatter(ROWS)

    def part_of(i):
        return pl.ds(pl.multiple_of(i * PART, 8), PART)

    copies = [
        remote(ax.at[part_of(at4(zq, 2))], rz.at[2], dev(dz=2)),
        remote(ax.at[part_of(at4(zq, 1))], rz.at[0], dev(dz=1)),
        remote(ax.at[part_of(at4(zq, 3))], rz.at[1], dev(dz=-1)),
    ]
    go(copies)

    def along_x(src, dst):
        return [
            remote(src.at[pl.ds(at4(x, d) * 4, 4)], dst.at[x], dev(dx=e))
            for d, e in ((2, 2), (1, 1), (3, -1))
        ]

    def along_y(src, dst):
        return [
            remote(src.at[:, at4(yl, d)], dst.at[:, yl], dev(dy=e))
            for d, e in ((2, 2), (1, 1), (3, -1))
        ]

    st_x = along_x(st, stm)
    st_y = along_y(stm, stx)

    @pl.when(is_vis)
    def _():
        go(st_x)
        stm[x] = st[pl.ds(x * 4, 4)]

    done(copies)
    az[...] = (ax[part_of(zq), :] + rz[0]) + (rz[1] + rz[2])

    ra, rb = pl.ds(0, 16), pl.ds(16, PART - 16)

    def along_far_z(src, rows):
        return [
            remote(src.at[rows], rzh.at[2, rows], dev(dz=8)),
            remote(src.at[rows], rzh.at[0, rows], dev(dz=4)),
            remote(src.at[rows], rzh.at[1, rows], dev(dz=-4)),
        ]

    def far_sum(own, rows):
        return (own[rows, :] + rzh[2, rows, :]) + (rzh[0, rows, :] + rzh[1, rows, :])

    far_a = remote(az.at[ra], ryh.at[ra], dev(dy=4))
    far_a.start()
    pl.semaphore_wait(far_sem, 2)
    z_b = along_far_z(az, rb)
    go(z_b)

    @pl.when(is_vis)
    def _():
        done(st_x)

    far_a.wait()
    ah[ra, :] = az[ra, :] + ryh[ra, :]
    z_a = along_far_z(ah, ra)
    go(z_a)

    @pl.when(is_vis)
    def _():
        go(st_y)
        stx[:, yl] = stm[:, yl]

    done(z_b)
    ah[rb, :] = far_sum(az, rb)
    far_b = remote(ah.at[rb], ryh.at[rb], dev(dy=4))
    far_b.start()

    t = jnp.full((1, 128), step_ref[0].astype(F32), F32)
    inv_one = 1.0 / (1.0 - jnp.exp(t * math.log(beta_one)))
    inv_two = 1.0 / (1.0 - jnp.exp(t * math.log(beta_two)))

    def blocks_of(k):
        rows = stx[:, :, k * SLOT : k * SLOT + SLOT, :].reshape(16 * SLOT, 128)
        return lax.dot_general(
            pick[...], rows, (((0,), (0,)), ((), ())), precision=HIGH, preferred_element_type=F32
        )

    @pl.when(is_vis)
    def _():
        done(st_y)
        for k in range(3):
            n_vis[k, 0:ROWS, :] = blocks_of(k)

    far_b.wait()
    tz[rb, :] = ah[rb, :] + ryh[rb, :]
    done(z_a)
    tz[ra, :] = far_sum(ah, ra)

    copies = [
        remote(tz, g4.at[zq], dev(dz=2)),
        remote(tz, g4.at[zq], dev(dz=1)),
        remote(tz, g4.at[zq], dev(dz=-1)),
    ]
    go(copies)
    g4[zq] = tz[...]
    done(copies)

    g_x = along_x(gx, gm)
    g_y = along_y(gm, gr)
    dec_over = remote(gdec, gdec, dev(dc=1))
    vis_over = remote(gr, gr, dev(dc=1))

    class Gather:
        def __init__(self, rows, top):
            up, down = pl.ds(0, top), pl.ds(top, rows - top)
            every = pl.ds(0, 4)

            def same(view, device):
                return remote(view, view, device)

            self.x = [same(wall.at[x, yl, up], dev(dx=d)) for d in (2, 1, -1)]
            self.y = [same(wall.at[x, yl, down], dev(dy=d)) for d in (2, 1, -1)]
            self.xy = [
                same(wall.at[:, yl, up], dev(dy=1)),
                same(wall.at[:, yl, up], dev(dy=-1)),
                same(wall.at[lo, yl, up], dev(dy=2)),
                same(wall.at[hi, yl, up], dev(dy=-2)),
            ]
            self.yx = [same(wall.at[x, :, down], dev(dx=d)) for d in (1, -1, 2)]
            self.over = [
                remote(wall.at[index], other.at[index], dev(dc=1))
                for index in (
                    (every, yl, up),
                    (x, every, down),
                    (every, q3, up),
                    (x3, every, down),
                    (every, q1, up),
                    (x1, every, down),
                    (lo, q2, up),
                    (hi, q2, up),
                    (x2, every, down),
                )
            ]

    mark = used[0]
    of_dec = Gather(DEC, 32)
    used[0] = mark
    of_vis = Gather(ROWS, CUT)

    def tail(rows, vision):
        mine, theirs = (of_vis, of_dec) if vision else (of_dec, of_vis)
        g = g4[...].reshape(PAD, 128)[0:rows]
        if vision:
            m, v, p = n_vis[1, 0:rows, :], n_vis[2, 0:rows, :], n_vis[0, 0:rows, :]
        else:
            gdec[...] = g
            dec_over.start()
            m, v, p = s_dec[1], s_dec[2], s_dec[0]
        wall[x, yl, 0:rows, :] = adamw(g, m, v, p, inv_one, inv_two)[2].astype(BF16)
        go(mine.x)
        go(mine.y)
        if vision:
            gx[...] = jnp.dot(pick[...], g, precision=HIGH, preferred_element_type=F32).reshape(
                16, SLOT, 128
            )
            go(g_x)
            gm[x] = gx[pl.ds(x * 4, 4)]
        done(mine.x)
        go(mine.xy)
        mine.over[0].start()
        done(mine.y)
        go(mine.yx)
        mine.over[1].start()
        if vision:
            done(g_x)
            go(g_y)
            gr[:, yl] = gm[:, yl]
            dec_over.wait_recv()
        m, v, p = adamw(gdec[...], s_dec[1], s_dec[2], s_dec[0], inv_one, inv_two)
        n_dec[0], n_dec[1], n_dec[2] = p, m, v
        if vision:
            done(g_y)
            vis_over.start()
        arrivals = (mine.xy[0], mine.yx[0], mine.xy[1], mine.yx[1], mine.xy[2], mine.xy[3], mine.yx[2])
        for a, b in zip(arrivals, mine.over[2:]):
            a.wait()
            b.start()
        if not vision:
            vis_over.wait_recv()
        for i in range(16):
            part = pl.ds(i * USED, USED)
            m, v, p = adamw(
                gr[i // 4, i % 4, 0:USED, :],
                s_vis[1, part, :],
                s_vis[2, part, :],
                s_vis[0, part, :],
                inv_one,
                inv_two,
            )
            n_vis[0, part, :] = p
            n_vis[1, part, :] = m
            n_vis[2, part, :] = v
        for c in mine.over:
            c.wait_send()
        for c in theirs.over:
            c.wait_recv()
        if vision:
            vis_over.wait_send()
        else:
            dec_over.wait_send()

    @pl.when(is_dec)
    def _():
        tail(DEC, False)

    @pl.when(is_vis)
    def _():
        tail(ROWS, True)

    assert (locals_used[0], used[0]) == (LOCALS, REMOTES), (locals_used, used)


def finish(
    n_dec, n_vis, mine, other, o_dp, o_dm, o_dv, o_dw, o_vp, o_vm, o_vv, o_vw, wide, dw, sems
):
    core = lax.rem(lax.axis_index("replica"), 2)
    pairs = [(n_dec.at[k], o) for k, o in enumerate((o_dp, o_dm, o_dv))]
    pairs += [(n_vis.at[k], o) for k, o in enumerate((o_vp, o_vm, o_vv))]
    copies = [pltpu.make_async_copy(a, b, sems.at[k]) for k, (a, b) in enumerate(pairs)]
    for c in copies:
        c.start()

    def weights(dec, vis):
        first = pltpu.make_async_copy(vis.reshape(16 * ROWS, 128), o_vw, sems.at[len(pairs)])
        first.start()
        for i in range(16):
            wide[i * DEC : i * DEC + DEC, :] = dec[i // 4, i % 4, 0:DEC, :].astype(F32)
        for j in range(DEC):
            dw[:, j * 128 : j * 128 + 128] = wide[pl.ds(j, 16, stride=DEC), :].astype(BF16)
        last = pltpu.make_async_copy(dw, o_dw, sems.at[len(pairs) + 1])
        last.start()
        first.wait()
        last.wait()

    @pl.when(core == 0)
    def _():
        weights(mine, other)

    @pl.when(core == 1)
    def _():
        weights(other, mine)

    for c in copies:
        c.wait()


def body(
    dec_grad,
    dec_master,
    dec_moment,
    dec_second,
    vis_grad,
    vis_owner,
    vis_master,
    vis_moment,
    vis_second,
    step_count,
):
    anywhere = pl.BlockSpec(memory_space=pl.ANY)
    sds = jax.ShapeDtypeStruct
    vmem = pltpu.VMEM
    inner_shape = [
        vmem((3, DEC, 128), F32),
        vmem((3, CAP, 128), F32),
        vmem((4, 4, ROWS, 128), BF16),
        vmem((4, 4, ROWS, 128), BF16),
    ]
    out_shape = [
        sds((DEC, 128), F32),
        sds((DEC, 128), F32),
        sds((DEC, 128), F32),
        sds((16, DEC * 128), BF16),
        sds((CAP, 128), F32),
        sds((CAP, 128), F32),
        sds((CAP, 128), F32),
        sds((16 * ROWS, 128), BF16),
    ]
    on_chip = pl.BlockSpec(memory_space=pltpu.VMEM)
    scratch = [
        vmem((16, DEC * 128), BF16),
        vmem((16, DEC * 128), BF16),
        vmem((16 * ROWS, 128), BF16),
        vmem((16 * ROWS, 128), BF16),
        vmem((3, DEC, 128), F32),
        vmem((3, CAP, 128), F32),
        vmem((4, 4, ROWS, 128), F32),
        vmem((3, 4, HALF, 128), F32),
        vmem((4, HALF, 128), F32),
        vmem((3, 4, HALF, 128), F32),
        vmem((4, HALF, 128), F32),
        vmem((3, HALF, 128), F32),
        vmem((3, HALF, 128), F32),
        vmem((PAD, 128), F32),
        vmem((3, PART, 128), F32),
        vmem((PART, 128), F32),
        vmem((PART, 128), F32),
        vmem((PART, 128), F32),
        vmem((3, PART, 128), F32),
        vmem((PART, 128), F32),
        vmem((4, PART, 128), F32),
        vmem((DEC, 128), F32),
        vmem((16, 3 * SLOT, 128), F32),
        vmem((4, 4, 3 * SLOT, 128), F32),
        vmem((4, 4, 3 * SLOT, 128), F32),
        vmem((16, SLOT, 128), F32),
        vmem((4, 4, SLOT, 128), F32),
        vmem((4, 4, SLOT, 128), F32),
        pltpu.SMEM((16 * ROWS,), jnp.int32),
        vmem((16 * SLOT, ROWS), F32),
        pltpu.SemaphoreType.DMA((LOCALS,)),
        pltpu.SemaphoreType.DMA((SENDS,)),
        pltpu.SemaphoreType.DMA((REMOTES,)),
        pltpu.SemaphoreType.REGULAR,
        pltpu.SemaphoreType.REGULAR,
    ]
    inner = pl.pallas_call(
        kernel,
        out_shape=inner_shape,
        in_specs=[pl.BlockSpec(memory_space=pltpu.SMEM)]
        + [pl.BlockSpec(memory_space=pltpu.HBM)] * 9,
        out_specs=[on_chip] * 4,
        scratch_shapes=scratch,
        compiler_params=pltpu.CompilerParams(collective_id=0, has_side_effects=True),
    )(
        step_count,
        vis_owner,
        dec_grad,
        vis_grad,
        dec_master.reshape(DEC, 128),
        dec_moment.reshape(DEC, 128),
        dec_second.reshape(DEC, 128),
        vis_master,
        vis_moment,
        vis_second,
    )
    outs = pl.pallas_call(
        finish,
        out_shape=out_shape,
        in_specs=[on_chip] * 4,
        out_specs=[anywhere] * 8,
        scratch_shapes=[
            vmem((16 * DEC, 128), F32),
            vmem((16, DEC * 128), BF16),
            pltpu.SemaphoreType.DMA((8,)),
        ],
    )(*[pltpu.with_memory_space_constraint(a, pltpu.VMEM) for a in inner])
    outs = list(outs)
    for i in range(3):
        outs[i] = outs[i].reshape(1, DEC * 128)
    return tuple(outs)


def solution(mesh):
    in_specs = (
        P(("replica", "shard"), None, None),
        P("shard", None),
        P("shard", None),
        P("shard", None),
        P(("replica", "shard"), None, None),
        P(),
        P("shard", None),
        P("shard", None),
        P("shard", None),
        P(),
    )
    out_specs = (
        P("shard", None),
        P("shard", None),
        P("shard", None),
        P(),
        P("shard", None),
        P("shard", None),
        P("shard", None),
        P(),
    )
    return jax.shard_map(body, mesh=mesh, in_specs=in_specs, out_specs=out_specs, check_vma=False)
```

```python
import itertools
import math

import jax
import jax.numpy as jnp
from jax import lax
from jax.experimental import pallas as pl
from jax.experimental.pallas import tpu as pltpu
from jax.sharding import PartitionSpec as P

beta_one = 0.9
beta_two = 0.999
learn_rate = 0.02
weight_decay = 0.1
epsilon = 1e-08

MESH = pl.DeviceIdType.MESH
F32 = jnp.float32
BF16 = jnp.bfloat16
HIGH = lax.Precision.HIGHEST

NX, NY, NZ = 4, 8, 16
Q = 4
ROWS = 80
DEC = 64
PAD = 96
HALF = ROWS // 2
CUT = 40
PART = PAD // 4
SLOT = 16
USED = 10
CAP = 160
LOCALS, REMOTES = 9, 65
SENDS = 24


def adamw(g, m, v, p, inv_one, inv_two):
    m = beta_one * m + (1.0 - beta_one) * g
    v = beta_two * v + (1.0 - beta_two) * g * g
    p = p - learn_rate * (m * inv_one / (jnp.sqrt(v * inv_two) + epsilon) + weight_decay * p)
    return m, v, p


def kernel(
    step_ref,
    own_ref,
    dec_grad,
    vis_grad,
    dec_p,
    dec_m,
    dec_v,
    vis_p,
    vis_m,
    vis_v,
    n_dec,
    n_vis,
    wall,
    other,
    a_dec,
    b_dec,
    a_vis,
    b_vis,
    s_dec,
    s_vis,
    acc,
    ry,
    ay,
    rx,
    ak,
    rx2,
    ry2,
    ax,
    rz,
    az,
    ryh,
    ah,
    rzh,
    tz,
    g4,
    gdec,
    st,
    stm,
    stx,
    gx,
    gm,
    gr,
    owner,
    pick,
    lsem,
    ssem,
    rsem,
    near_sem,
    far_sem,
):
    rep, sh = lax.axis_index("replica"), lax.axis_index("shard")
    core = lax.rem(rep, 2)
    z = lax.rem(rep // 2, NZ)
    yl = lax.rem(sh, Q)
    y = (rep // (2 * NZ)) * Q + yl
    x = sh // Q
    zq = lax.rem(z, 4)

    def dev(dx=0, dy=0, dz=0, dc=0):
        xx = lax.rem(x + dx + NX, NX)
        yy = lax.rem(y + dy + NY, NY)
        zz = lax.rem(z + dz + NZ, NZ)
        cc = lax.rem(core + dc, 2)
        return ((yy // Q) * NZ + zz) * 2 + cc, xx * Q + lax.rem(yy, Q)

    def at4(i, d):
        return lax.rem(i + d + 4, 4)

    used = [0]

    def remote(src, dst, target):
        k = used[0]
        used[0] += 1
        return pltpu.make_async_remote_copy(
            src_ref=src,
            dst_ref=dst,
            send_sem=ssem.at[k % SENDS],
            recv_sem=rsem.at[k],
            device_id=target,
            device_id_type=MESH,
        )

    locals_used = [0]

    def local(src, dst):
        k = locals_used[0]
        locals_used[0] += 1
        return pltpu.make_async_copy(src, dst, lsem.at[k])

    def go(copies):
        for c in copies:
            c.start()

    def done(copies):
        for c in copies:
            c.wait()

    is_dec, is_vis = core == 0, core == 1

    load_dec = local(dec_grad.at[0], a_dec)
    load_vis = local(vis_grad.at[0], a_vis)
    load_maps = [local(own_ref, owner)]
    load_state = [
        local(src, dst)
        for src, dst in (
            (dec_p, s_dec.at[0]),
            (dec_m, s_dec.at[1]),
            (dec_v, s_dec.at[2]),
            (vis_p, s_vis.at[0]),
            (vis_m, s_vis.at[1]),
            (vis_v, s_vis.at[2]),
        )
    ]

    @pl.when(is_dec)
    def _():
        load_dec.start()

    @pl.when(is_vis)
    def _():
        load_vis.start()

    go(load_maps)
    go(load_state)

    friends = [dev(dc=1)]
    friends += [dev(dx=d) for d in (1, -1, 2)]
    friends += [dev(dy=d) for d in (1, -1, 2, -2)]
    friends += [dev(dz=d) for d in (1, -1, 2, -2)]
    barrier = pltpu.get_barrier_semaphore()
    for friend in friends:
        pl.semaphore_signal(barrier, inc=1, device_id=friend, device_id_type=MESH)
    pl.semaphore_wait(barrier, len(friends))

    for d in (2, -2):
        pl.semaphore_signal(near_sem, inc=1, device_id=dev(dz=d), device_id_type=MESH)

    send_vis = remote(vis_grad.at[0], b_vis, dev(dc=1))
    send_dec = remote(dec_grad.at[0], b_dec, dev(dc=1))

    @pl.when(is_dec)
    def _():
        send_vis.start()
        load_dec.wait()
        send_dec.wait_recv()

        @pl.loop(0, DEC)
        def _(j):
            at = pl.multiple_of(j * 128, 128)
            block = a_dec[:, pl.ds(at, 128)].astype(F32) + b_dec[:, pl.ds(at, 128)].astype(F32)
            acc.reshape(16 * ROWS, 128)[pl.ds(j, 16, stride=ROWS), :] = block

        send_vis.wait_send()

    @pl.when(is_vis)
    def _():
        send_dec.start()
        load_vis.wait()
        send_vis.wait_recv()

        for i in range(16):
            part = pl.ds(i * ROWS, ROWS)
            acc[i // 4, i % 4] = a_vis[part, :].astype(F32) + b_vis[part, :].astype(F32)
        send_dec.wait_send()

    def prepare():
        done(load_state)
        done(load_maps)
        for i in range(16):
            for k in range(3):
                st[i, k * SLOT : k * SLOT + SLOT, :] = jnp.zeros((SLOT, 128), F32)
                st[i, k * SLOT : k * SLOT + USED, :] = s_vis[k, i * USED : i * USED + USED, :]
        lane = lax.broadcasted_iota(jnp.int32, (1, ROWS), 1)
        own = lax.fori_loop(
            0,
            ROWS,
            lambda i, v: jnp.where(lane == i, owner[sh * ROWS + i], v),
            jnp.zeros((1, ROWS), jnp.int32),
        )
        one_hot = (lax.broadcasted_iota(jnp.int32, (16, ROWS), 0) == own).astype(F32)
        before = (
            lax.broadcasted_iota(jnp.int32, (ROWS, ROWS), 0)
            < lax.broadcasted_iota(jnp.int32, (ROWS, ROWS), 1)
        ).astype(F32)
        count = jnp.dot(one_hot, before, preferred_element_type=F32)
        position = jnp.sum(one_hot * count, axis=0, keepdims=True)
        key = own * SLOT + position.astype(jnp.int32)
        pick[...] = (lax.broadcasted_iota(jnp.int32, (16 * SLOT, ROWS), 0) == key).astype(F32)

    q1, q2, q3 = at4(yl, 1), at4(yl, 2), at4(yl, 3)
    x1, x2, x3 = at4(x, 1), at4(x, 2), at4(x, 3)
    lo, hi = pl.ds(0, 2), pl.ds(2, 2)

    def scatter(rows):
        half = rows // 2
        one, two, part = pl.ds(0, half), pl.ds(half, half), pl.ds(0, half)
        first_y = [
            remote(acc.at[lo, q2, one], ry.at[2, lo, part], dev(dy=2)),
            remote(acc.at[hi, q2, one], ry.at[2, hi, part], dev(dy=-2)),
            remote(acc.at[:, q1, one], ry.at[0, :, part], dev(dy=1)),
            remote(acc.at[:, q3, one], ry.at[1, :, part], dev(dy=-1)),
        ]
        first_x = [
            remote(acc.at[x2, :, two], rx.at[2, :, part], dev(dx=2)),
            remote(acc.at[x1, :, two], rx.at[0, :, part], dev(dx=1)),
            remote(acc.at[x3, :, two], rx.at[1, :, part], dev(dx=-1)),
        ]
        second_x = [
            remote(ay.at[x2, part], rx2.at[2, part], dev(dx=2)),
            remote(ay.at[x1, part], rx2.at[0, part], dev(dx=1)),
            remote(ay.at[x3, part], rx2.at[1, part], dev(dx=-1)),
        ]
        second_y = [
            remote(ak.at[q2, part], ry2.at[2, part], dev(dy=2)),
            remote(ak.at[q1, part], ry2.at[0, part], dev(dy=1)),
            remote(ak.at[q3, part], ry2.at[1, part], dev(dy=-1)),
        ]
        for a, b in itertools.zip_longest(first_y, first_x):
            a.start()
            if b is not None:
                b.start()
        pl.semaphore_wait(near_sem, 2)
        for d in (4, -4):
            pl.semaphore_signal(far_sem, inc=1, device_id=dev(dz=d), device_id_type=MESH)
        if rows == ROWS:
            prepare()
        else:
            done(load_state)
            done(load_maps)
        done(first_y)
        for i in range(NX):
            ay[i, part, :] = (acc[i, yl, one, :] + ry[0, i, part, :]) + (
                ry[1, i, part, :] + ry[2, i, part, :]
            )
        go(second_x)
        done(first_x)
        for i in range(Q):
            ak[i, part, :] = (acc[x, i, two, :] + rx[0, i, part, :]) + (
                rx[1, i, part, :] + rx[2, i, part, :]
            )
        go(second_y)
        done(second_x)
        ax[one, :] = (ay[x, part, :] + rx2[0, part, :]) + (rx2[1, part, :] + rx2[2, part, :])
        done(second_y)
        ax[two, :] = (ak[yl, part, :] + ry2[0, part, :]) + (ry2[1, part, :] + ry2[2, part, :])
        ax[rows:PAD, :] = jnp.zeros((PAD - rows, 128), F32)

    mark = used[0]

    @pl.when(is_dec)
    def _():
        scatter(DEC)

    used[0] = mark

    @pl.when(is_vis)
    def _():
        scatter(ROWS)

    def part_of(i):
        return pl.ds(pl.multiple_of(i * PART, 8), PART)

    copies = [
        remote(ax.at[part_of(at4(zq, 2))], rz.at[2], dev(dz=2)),
        remote(ax.at[part_of(at4(zq, 1))], rz.at[0], dev(dz=1)),
        remote(ax.at[part_of(at4(zq, 3))], rz.at[1], dev(dz=-1)),
    ]
    go(copies)

    def along_x(src, dst):
        return [
            remote(src.at[pl.ds(at4(x, d) * 4, 4)], dst.at[x], dev(dx=e))
            for d, e in ((2, 2), (1, 1), (3, -1))
        ]

    def along_y(src, dst):
        return [
            remote(src.at[:, at4(yl, d)], dst.at[:, yl], dev(dy=e))
            for d, e in ((2, 2), (1, 1), (3, -1))
        ]

    st_x = along_x(st, stm)
    st_y = along_y(stm, stx)

    @pl.when(is_vis)
    def _():
        go(st_x)
        stm[x] = st[pl.ds(x * 4, 4)]

    done(copies)
    az[...] = (ax[part_of(zq), :] + rz[0]) + (rz[1] + rz[2])

    ra, rb = pl.ds(0, 16), pl.ds(16, PART - 16)

    def along_far_z(src, rows):
        return [
            remote(src.at[rows], rzh.at[2, rows], dev(dz=8)),
            remote(src.at[rows], rzh.at[0, rows], dev(dz=4)),
            remote(src.at[rows], rzh.at[1, rows], dev(dz=-4)),
        ]

    def far_sum(own, rows):
        return (own[rows, :] + rzh[2, rows, :]) + (rzh[0, rows, :] + rzh[1, rows, :])

    far_a = remote(az.at[ra], ryh.at[ra], dev(dy=4))
    far_a.start()
    pl.semaphore_wait(far_sem, 2)
    z_b = along_far_z(az, rb)
    go(z_b)

    @pl.when(is_vis)
    def _():
        done(st_x)

    far_a.wait()
    ah[ra, :] = az[ra, :] + ryh[ra, :]
    z_a = along_far_z(ah, ra)
    go(z_a)

    @pl.when(is_vis)
    def _():
        go(st_y)
        stx[:, yl] = stm[:, yl]

    done(z_b)
    ah[rb, :] = far_sum(az, rb)
    far_b = remote(ah.at[rb], ryh.at[rb], dev(dy=4))
    far_b.start()

    t = jnp.full((1, 128), step_ref[0].astype(F32), F32)
    inv_one = 1.0 / (1.0 - jnp.exp(t * math.log(beta_one)))
    inv_two = 1.0 / (1.0 - jnp.exp(t * math.log(beta_two)))

    def blocks_of(k):
        rows = stx[:, :, k * SLOT : k * SLOT + SLOT, :].reshape(16 * SLOT, 128)
        return lax.dot_general(
            pick[...], rows, (((0,), (0,)), ((), ())), precision=HIGH, preferred_element_type=F32
        )

    @pl.when(is_vis)
    def _():
        done(st_y)
        for k in range(3):
            n_vis[k, 0:ROWS, :] = blocks_of(k)

    far_b.wait()
    tz[rb, :] = ah[rb, :] + ryh[rb, :]
    done(z_a)
    tz[ra, :] = far_sum(ah, ra)

    copies = [
        remote(tz, g4.at[zq], dev(dz=2)),
        remote(tz, g4.at[zq], dev(dz=1)),
        remote(tz, g4.at[zq], dev(dz=-1)),
    ]
    go(copies)
    g4[zq] = tz[...]
    done(copies)

    g_x = along_x(gx, gm)
    g_y = along_y(gm, gr)
    dec_over = remote(gdec, gdec, dev(dc=1))
    vis_over = remote(gr, gr, dev(dc=1))

    class Gather:
        def __init__(self, rows, top):
            up, down = pl.ds(0, top), pl.ds(top, rows - top)
            every = pl.ds(0, 4)

            def same(view, device):
                return remote(view, view, device)

            self.x = [same(wall.at[x, yl, up], dev(dx=d)) for d in (2, 1, -1)]
            self.y = [same(wall.at[x, yl, down], dev(dy=d)) for d in (2, 1, -1)]
            self.xy = [
                same(wall.at[:, yl, up], dev(dy=1)),
                same(wall.at[:, yl, up], dev(dy=-1)),
                same(wall.at[lo, yl, up], dev(dy=2)),
                same(wall.at[hi, yl, up], dev(dy=-2)),
            ]
            self.yx = [same(wall.at[x, :, down], dev(dx=d)) for d in (1, -1, 2)]
            self.over = [
                remote(wall.at[index], other.at[index], dev(dc=1))
                for index in (
                    (every, yl, up),
                    (x, every, down),
                    (every, q3, up),
                    (x3, every, down),
                    (every, q1, up),
                    (x1, every, down),
                    (lo, q2, up),
                    (hi, q2, up),
                    (x2, every, down),
                )
            ]

    mark = used[0]
    of_dec = Gather(DEC, 32)
    used[0] = mark
    of_vis = Gather(ROWS, CUT)

    def tail(rows, vision):
        mine, theirs = (of_vis, of_dec) if vision else (of_dec, of_vis)
        g = g4[...].reshape(PAD, 128)[0:rows]
        if vision:
            m, v, p = n_vis[1, 0:rows, :], n_vis[2, 0:rows, :], n_vis[0, 0:rows, :]
        else:
            gdec[...] = g
            dec_over.start()
            m, v, p = s_dec[1], s_dec[2], s_dec[0]
        wall[x, yl, 0:rows, :] = adamw(g, m, v, p, inv_one, inv_two)[2].astype(BF16)
        go(mine.x)
        go(mine.y)
        if vision:
            gx[...] = jnp.dot(pick[...], g, precision=HIGH, preferred_element_type=F32).reshape(
                16, SLOT, 128
            )
            go(g_x)
            gm[x] = gx[pl.ds(x * 4, 4)]
        done(mine.x)
        go(mine.xy)
        mine.over[0].start()
        done(mine.y)
        go(mine.yx)
        mine.over[1].start()
        if vision:
            done(g_x)
            go(g_y)
            gr[:, yl] = gm[:, yl]
            dec_over.wait_recv()
        m, v, p = adamw(gdec[...], s_dec[1], s_dec[2], s_dec[0], inv_one, inv_two)
        n_dec[0], n_dec[1], n_dec[2] = p, m, v
        if vision:
            done(g_y)
            vis_over.start()
        arrivals = (mine.xy[0], mine.yx[0], mine.xy[1], mine.yx[1], mine.xy[2], mine.xy[3], mine.yx[2])
        for a, b in zip(arrivals, mine.over[2:]):
            a.wait()
            b.start()
        if not vision:
            vis_over.wait_recv()
        for i in range(16):
            part = pl.ds(i * USED, USED)
            m, v, p = adamw(
                gr[i // 4, i % 4, 0:USED, :],
                s_vis[1, part, :],
                s_vis[2, part, :],
                s_vis[0, part, :],
                inv_one,
                inv_two,
            )
            n_vis[0, part, :] = p
            n_vis[1, part, :] = m
            n_vis[2, part, :] = v
        for c in mine.over:
            c.wait_send()
        for c in theirs.over:
            c.wait_recv()
        if vision:
            vis_over.wait_send()
        else:
            dec_over.wait_send()

    @pl.when(is_dec)
    def _():
        tail(DEC, False)

    @pl.when(is_vis)
    def _():
        tail(ROWS, True)

    assert (locals_used[0], used[0]) == (LOCALS, REMOTES), (locals_used, used)


def finish(
    n_dec, n_vis, mine, other, o_dp, o_dm, o_dv, o_dw, o_vp, o_vm, o_vv, o_vw, wide, dw, sems
):
    core = lax.rem(lax.axis_index("replica"), 2)
    pairs = [(n_dec.at[k], o) for k, o in enumerate((o_dp, o_dm, o_dv))]
    pairs += [(n_vis.at[k], o) for k, o in enumerate((o_vp, o_vm, o_vv))]
    copies = [pltpu.make_async_copy(a, b, sems.at[k]) for k, (a, b) in enumerate(pairs)]
    for c in copies:
        c.start()

    def weights(dec, vis):
        first = pltpu.make_async_copy(vis.reshape(16 * ROWS, 128), o_vw, sems.at[len(pairs)])
        first.start()
        for i in range(16):
            wide[i * DEC : i * DEC + DEC, :] = dec[i // 4, i % 4, 0:DEC, :].astype(F32)
        for j in range(DEC):
            dw[:, j * 128 : j * 128 + 128] = wide[pl.ds(j, 16, stride=DEC), :].astype(BF16)
        last = pltpu.make_async_copy(dw, o_dw, sems.at[len(pairs) + 1])
        last.start()
        first.wait()
        last.wait()

    @pl.when(core == 0)
    def _():
        weights(mine, other)

    @pl.when(core == 1)
    def _():
        weights(other, mine)

    for c in copies:
        c.wait()


def body(
    dec_grad,
    dec_master,
    dec_moment,
    dec_second,
    vis_grad,
    vis_owner,
    vis_master,
    vis_moment,
    vis_second,
    step_count,
):
    anywhere = pl.BlockSpec(memory_space=pl.ANY)
    sds = jax.ShapeDtypeStruct
    vmem = pltpu.VMEM
    inner_shape = [
        vmem((3, DEC, 128), F32),
        vmem((3, CAP, 128), F32),
        vmem((4, 4, ROWS, 128), BF16),
        vmem((4, 4, ROWS, 128), BF16),
    ]
    out_shape = [
        sds((DEC, 128), F32),
        sds((DEC, 128), F32),
        sds((DEC, 128), F32),
        sds((16, DEC * 128), BF16),
        sds((CAP, 128), F32),
        sds((CAP, 128), F32),
        sds((CAP, 128), F32),
        sds((16 * ROWS, 128), BF16),
    ]
    on_chip = pl.BlockSpec(memory_space=pltpu.VMEM)
    scratch = [
        vmem((16, DEC * 128), BF16),
        vmem((16, DEC * 128), BF16),
        vmem((16 * ROWS, 128), BF16),
        vmem((16 * ROWS, 128), BF16),
        vmem((3, DEC, 128), F32),
        vmem((3, CAP, 128), F32),
        vmem((4, 4, ROWS, 128), F32),
        vmem((3, 4, HALF, 128), F32),
        vmem((4, HALF, 128), F32),
        vmem((3, 4, HALF, 128), F32),
        vmem((4, HALF, 128), F32),
        vmem((3, HALF, 128), F32),
        vmem((3, HALF, 128), F32),
        vmem((PAD, 128), F32),
        vmem((3, PART, 128), F32),
        vmem((PART, 128), F32),
        vmem((PART, 128), F32),
        vmem((PART, 128), F32),
        vmem((3, PART, 128), F32),
        vmem((PART, 128), F32),
        vmem((4, PART, 128), F32),
        vmem((DEC, 128), F32),
        vmem((16, 3 * SLOT, 128), F32),
        vmem((4, 4, 3 * SLOT, 128), F32),
        vmem((4, 4, 3 * SLOT, 128), F32),
        vmem((16, SLOT, 128), F32),
        vmem((4, 4, SLOT, 128), F32),
        vmem((4, 4, SLOT, 128), F32),
        pltpu.SMEM((16 * ROWS,), jnp.int32),
        vmem((16 * SLOT, ROWS), F32),
        pltpu.SemaphoreType.DMA((LOCALS,)),
        pltpu.SemaphoreType.DMA((SENDS,)),
        pltpu.SemaphoreType.DMA((REMOTES,)),
        pltpu.SemaphoreType.REGULAR,
        pltpu.SemaphoreType.REGULAR,
    ]
    inner = pl.pallas_call(
        kernel,
        out_shape=inner_shape,
        in_specs=[pl.BlockSpec(memory_space=pltpu.SMEM)]
        + [pl.BlockSpec(memory_space=pltpu.HBM)] * 9,
        out_specs=[on_chip] * 4,
        scratch_shapes=scratch,
        compiler_params=pltpu.CompilerParams(collective_id=0, has_side_effects=True),
    )(
        step_count,
        vis_owner,
        dec_grad,
        vis_grad,
        dec_master.reshape(DEC, 128),
        dec_moment.reshape(DEC, 128),
        dec_second.reshape(DEC, 128),
        vis_master,
        vis_moment,
        vis_second,
    )
    outs = pl.pallas_call(
        finish,
        out_shape=out_shape,
        in_specs=[on_chip] * 4,
        out_specs=[anywhere] * 8,
        scratch_shapes=[
            vmem((16 * DEC, 128), F32),
            vmem((16, DEC * 128), BF16),
            pltpu.SemaphoreType.DMA((8,)),
        ],
    )(*[pltpu.with_memory_space_constraint(a, pltpu.VMEM) for a in inner])
    outs = list(outs)
    for i in range(3):
        outs[i] = outs[i].reshape(1, DEC * 128)
    return tuple(outs)


def solution(mesh):
    in_specs = (
        P(("replica", "shard"), None, None),
        P("shard", None),
        P("shard", None),
        P("shard", None),
        P(("replica", "shard"), None, None),
        P(),
        P("shard", None),
        P("shard", None),
        P("shard", None),
        P(),
    )
    out_specs = (
        P("shard", None),
        P("shard", None),
        P("shard", None),
        P(),
        P("shard", None),
        P("shard", None),
        P("shard", None),
        P(),
    )
    return jax.shard_map(body, mesh=mesh, in_specs=in_specs, out_specs=out_specs, check_vma=False)
```
